128 devices in a mesh: gx: 8 (over z, core), gy: 16 (over y, x).
Axes of the slice: x: 4, y: 4, z: 4, core: 2. Of those that a mesh axis runs over, the one named last changes fastest.
Arguments:
- item_table: bfloat16 [1048576, 256], P(('gx', 'gy')), may hold values from -0.625 to 0.625
- bilinear: bfloat16 [256, 1024], replicated, may hold values from -0.375 to 0.375
- requests: int32 [128, 128, 64], P(('gx', 'gy')), may hold values from -1 to 8191, as said below
- history: int32 [32768, 50], P(('gx', 'gy')), may hold values from 0 to 8191, as said below
- lengths: int32 [32768], P(('gx', 'gy')), may hold values from 10 to 50
- init_logits: float32 [32768, 50, 4], P(('gx', 'gy')), may hold values from -6 to 6
- interest_grad: float32 [32768, 4, 256], P(('gx', 'gy')), may hold values from -6 to 6
Outputs:
- interests: bfloat16 [32768, 4, 256], P(('gx', 'gy'))
- table_grad: float32 [1048576, 256], P(('gx', 'gy'))
The draws below stay inside these ranges and needn't reach their ends.
Inputs may be any that keep to these rules, and one draw needn't show every extreme that they name: requests[r, o, c] is a row of table shard o asked by device r in slot c, or -1 for an unused slot; the used slots of a list come first, hold distinct rows, and number at least one; a few shards have full lists (64 used slots) from every device. history[u, l] = o * 64 + c names a used slot c of list o of the device holding user u (users are laid out 256 a device).
All inputs are finite; a program needn't handle non-finite values.
Results may differ from the reference program's by a relative error of at most 0.015.
Values may be sent and summed in bfloat16 or wider, within the bound.
A program may use at most 192 MiB of HBM per device.

```python
import jax
import jax.numpy as jnp
from jax import lax

D = 256
INTERESTS = 4
HIST_LEN = 50
ITERS = 3
ROWS_DEV = 8192
CAP = 64
USERS_DEV = 256
OWNERS = 128
USERS = 32768
ITEMS = 1048576


def request_layout(key):
    keys = jax.random.split(jax.random.fold_in(key, 11), 5)
    popular = jax.random.permutation(keys[0], OWNERS) < 4
    drawn = jax.random.randint(keys[1], (OWNERS, OWNERS), CAP // 2, CAP + 1)
    counts = jnp.where(popular[None, :], CAP, drawn).astype(jnp.int32)
    offset = jax.random.randint(keys[2], (OWNERS, OWNERS, 1), 0, ROWS_DEV)
    stride = 2 * jax.random.randint(keys[3], (OWNERS, OWNERS, 1), 0, ROWS_DEV // 2) + 1
    slot_ids = jnp.arange(CAP, dtype=jnp.int32)[None, None, :]
    asked_rows = (offset + slot_ids * stride) % ROWS_DEV
    requests = jnp.where(slot_ids < counts[:, :, None], asked_rows, -1).astype(jnp.int32)
    totals = jnp.sum(counts, axis=1)
    ends = jnp.cumsum(counts, axis=1)
    starts = ends - counts
    picks = jax.random.randint(keys[4], (OWNERS, USERS_DEV * HIST_LEN), 0, totals[:, None])
    owner_ids = jax.vmap(lambda edge, value: jnp.searchsorted(edge, value, side='right'))(ends, picks).astype(jnp.int32)
    ranks = picks - jnp.take_along_axis(starts, owner_ids, axis=1)
    history = (owner_ids * CAP + ranks).astype(jnp.int32).reshape(OWNERS * USERS_DEV, HIST_LEN)
    return (requests, history)


def draw_requests(key, part):
    return request_layout(key)[0]


def draw_history(key, part):
    return request_layout(key)[1]


def touch_ends(array, stream_key, smallest, largest):
    shape = array.shape
    spot = [jax.random.randint(jax.random.fold_in(stream_key, axis), (), 0, shape[axis]) for axis in range(len(shape))]
    array = array.at[tuple(spot)].set(smallest)
    longest = shape.index(max(shape))
    spot[longest] = (spot[longest] + 1) % shape[longest]
    return array.at[tuple(spot)].set(largest)


def steps_of(rng, extent, shards, low, high):
    gain = 1.0
    for axis_at, blocks in shards:
        steps = jax.random.uniform(jax.random.fold_in(jax.random.fold_in(rng, 6), axis_at), (blocks,), jnp.float32, low / len(shards), high / len(shards))
        gain = gain * jnp.repeat(jnp.exp(steps), extent[axis_at] // blocks).reshape((-1,) + (1,) * (len(extent) - 1 - axis_at))
    return gain


def normal_values(stream_key, shape, deviation, most, pieces=(), kind=jnp.bfloat16):
    values = jax.random.normal(stream_key, shape, jnp.float32) * deviation
    if len(pieces) > 0:
        values = steps_of(stream_key, shape, pieces, -0.22, 0.18) * values
    return jnp.clip(values, min=-most, max=most).astype(kind)


def setup_inputs(seed: int = 0) -> dict:
    key_list = jax.random.split(jax.random.key(seed), 8)
    return {
        "item_table": normal_values(key_list[0], (ITEMS, D), 0.1, 0.625, ((0, 128),)),
        "bilinear": normal_values(key_list[1], (D, INTERESTS * D), D ** -0.5, 0.375),
        "requests": draw_requests(jax.random.fold_in(key_list[7], 71), 0),
        "history": draw_history(jax.random.fold_in(key_list[7], 71), 0),
        "lengths": touch_ends(jax.random.randint(key_list[4], (USERS,), max(1, HIST_LEN // 5), HIST_LEN + 1), jax.random.fold_in(key_list[4], 1), max(1, HIST_LEN // 5), HIST_LEN).astype(jnp.int32),
        "init_logits": normal_values(key_list[5], (USERS, HIST_LEN, INTERESTS), 1.0, 6.0, ((0, 128),), jnp.float32),
        "interest_grad": normal_values(key_list[6], (USERS, INTERESTS, D), 1.0, 6.0, ((0, 128),), jnp.float32),
    }


squash_eps = 1e-06

def route_interests(behavior_rows, bilinear, lengths, init_logits):
    users_here, hist_count, feature_width = behavior_rows.shape
    interest_count = init_logits.shape[2]
    remapped_values = jnp.dot(behavior_rows.reshape(users_here * hist_count, feature_width), bilinear, preferred_element_type=jnp.float32)
    remapped_values = remapped_values.astype(jnp.bfloat16).reshape(users_here, hist_count, interest_count, feature_width)
    positions = lax.broadcasted_iota(jnp.int32, (users_here, hist_count), 1)
    live_mask = (positions < lengths[:, None]).astype(jnp.float32)
    logits = init_logits
    interest_capsule = None
    for turn_no in range(ITERS):
        exponent = jnp.exp(logits)
        coupling_weight = exponent / lax.optimization_barrier(jnp.sum(exponent, axis=2, keepdims=True)) * live_mask[:, :, None]
        weighted_total = jnp.einsum('rmq,rmqs->rqs', coupling_weight.astype(jnp.bfloat16), remapped_values, preferred_element_type=jnp.float32)
        norm_sq = lax.optimization_barrier(jnp.sum(weighted_total * weighted_total, axis=2, keepdims=True))
        interest_capsule = weighted_total * jnp.sqrt(norm_sq + squash_eps) / (1.0 + norm_sq)
        if turn_no + 1 < ITERS:
            routing_agreement_score = jnp.einsum('mazc,mzc->maz', remapped_values, interest_capsule.astype(jnp.bfloat16), preferred_element_type=jnp.float32)
            logits = logits + routing_agreement_score
    return interest_capsule

def reference(item_table, bilinear, requests, history, lengths, init_logits, interest_grad):
    feature_width = item_table.shape[1]
    flattened_request_list = requests.reshape(OWNERS, OWNERS * CAP)

    def per_device(carried, block_no):
        start = block_no * USERS_DEV
        history_item_block = lax.dynamic_slice_in_dim(history, start, USERS_DEV, 0)
        length_block = lax.dynamic_slice_in_dim(lengths, start, USERS_DEV, 0)
        logit_block = lax.dynamic_slice_in_dim(init_logits, start, USERS_DEV, 0)
        grad_block = lax.dynamic_slice_in_dim(interest_grad, start, USERS_DEV, 0)
        own_list = lax.dynamic_index_in_dim(flattened_request_list, block_no, 0, keepdims=False)
        local_table_rows = jnp.take(own_list, history_item_block.reshape(-1), axis=0)
        item_ids = (history_item_block.reshape(-1) // CAP * ROWS_DEV + local_table_rows).astype(jnp.int32)
        behavior_rows = jnp.take(item_table, item_ids, axis=0).reshape(USERS_DEV, HIST_LEN, feature_width)
        interest_capsule, pullback = jax.vjp(lambda given: route_interests(given, bilinear, length_block, logit_block), behavior_rows)
        row_grad, = pullback(grad_block)
        carried = carried.at[item_ids].add(row_grad.reshape(-1, feature_width).astype(jnp.float32))
        return (carried, interest_capsule.astype(jnp.bfloat16))
    empty = jnp.zeros((ITEMS, feature_width), jnp.float32)
    table_grad, capsules = lax.scan(per_device, empty, jnp.arange(OWNERS, dtype=jnp.int32))
    return (capsules.reshape(USERS, INTERESTS, feature_width), table_grad)
```

```python
import functools

import jax
import jax.numpy as jnp
from jax import lax
from jax.experimental import pallas as pl
from jax.experimental.pallas import tpu as pltpu
from jax.sharding import PartitionSpec as P

ITERS = 3
EPS = 1e-06
LP = 64
UG = 8
HALF = 128
MIB = 1024 * 1024
F32 = jnp.float32
BF16 = jnp.bfloat16


def vmem():
    return pl.BlockSpec(memory_space=pltpu.VMEM)


def smem():
    return pl.BlockSpec(memory_space=pltpu.SMEM)


def two(i):
    return pl.ds(pl.multiple_of(2 * i, 2), 2)


def split_rows(src, dst, rows, step=512):
    def body(c, carry):
        at = pl.multiple_of(c * step, step)
        for h in range(2):
            dst[pl.ds(2 * at + h, step, stride=2), :] = src[
                pl.ds(at, step), h * HALF : (h + 1) * HALF
            ].astype(F32)
        return carry

    lax.fori_loop(0, rows // step, body, 0)


def fetch_kernel(slots, ids, table, out, wide, stage):
    rows = table.shape[0]
    split_rows(table, wide, rows)

    def body(c, carry):
        for j in range(slots):
            stage[pl.ds(2 * j, 2), :] = wide[two(ids[c * slots + j]), :]
        out[pl.ds(pl.multiple_of(c * 2 * slots, 2 * slots), 2 * slots), :] = stage[...].astype(BF16)
        return carry

    lax.fori_loop(0, ids.shape[0] // slots, body, 0)


def fetch_rows(ids, table, slots):
    rows = table.shape[0]
    return pl.pallas_call(
        functools.partial(fetch_kernel, slots),
        name="fetch_rows",
        out_shape=jax.ShapeDtypeStruct((2 * ids.shape[0], HALF), BF16),
        in_specs=[smem(), vmem()],
        out_specs=vmem(),
        scratch_shapes=[pltpu.VMEM((2 * rows, HALF), F32), pltpu.VMEM((2 * slots, HALF), F32)],
        compiler_params=pltpu.CompilerParams(vmem_limit_bytes=40 * MIB),
    )(ids, table)


def return_kernel(slots, ids, grads, out, total, stage):
    step = pl.program_id(0)
    feed = ids.shape[0] * 2 // grads.shape[0]
    chunk = grads.shape[0]

    @pl.when(step == 0)
    def _():
        def clear(c, carry):
            total[pl.ds(pl.multiple_of(c * 512, 512), 512), :] = jnp.zeros((512, HALF), F32)
            return carry

        lax.fori_loop(0, (total.shape[0] - 16) // 512, clear, 0)

    @pl.when(step < feed)
    def _():
        stage[...] = grads[...].astype(F32)

        def body(c, carry):
            for b in range(2):
                base = c * 64 + b * 32
                at = [two(ids[step * (chunk // 2) + base + j]) for j in range(32)]
                held = [total[at[j], :] for j in range(32)]
                for j in range(32):
                    total[at[j], :] = held[j] + stage[two(base + j), :]
            return carry

        lax.fori_loop(0, chunk // 128, body, 0)

    @pl.when(step >= feed)
    def _():
        rows = out.shape[0]
        at = pl.multiple_of((step - feed) * 2 * rows, 2 * rows)
        for h in range(2):
            out[:, h * HALF : (h + 1) * HALF] = total[pl.ds(at + h, rows, stride=2), :]


def return_rows(ids, grads, rows, slots):
    feed = 8
    drain = 8
    chunk = grads.shape[0] // feed
    return pl.pallas_call(
        functools.partial(return_kernel, slots),
        name="return_rows",
        grid=(feed + drain,),
        out_shape=jax.ShapeDtypeStruct((rows, 2 * HALF), F32),
        in_specs=[smem(), pl.BlockSpec((chunk, HALF), lambda i: (jnp.minimum(i, feed - 1), 0))],
        out_specs=pl.BlockSpec((rows // drain, 2 * HALF), lambda i: (jnp.maximum(i - feed, 0), 0)),
        scratch_shapes=[pltpu.VMEM((2 * rows + 16, HALF), F32), pltpu.VMEM((chunk, HALF), F32)],
        compiler_params=pltpu.CompilerParams(vmem_limit_bytes=40 * MIB),
    )(ids, grads)


def route_kernel(
    interests, hist_len,
    slots, fetched, bilinear, first_logits, live, cotangent, same,
    capsules, slot_grads,
    wide, rows, stage, logits, w0, w1, w2, z0, z1, pooled, q0, q1, g0, g1, g2, s0, s1, s2,
    same_buf, same_sem,
):
    groups = live.shape[0]
    width = UG * LP
    lines = interests * UG
    feature = rows.shape[1]

    def nt(a, b):
        return lax.dot_general(a, b, (((1,), (1,)), ((), ())), preferred_element_type=F32)

    def tn(a, b):
        return lax.dot_general(a, b, (((0,), (0,)), ((), ())), preferred_element_type=F32)

    def block(g):
        return rows[pl.ds(pl.multiple_of(g * width, width), width), :]

    def lanes(ref, g):
        return ref.at[pl.ds(pl.multiple_of(g * lines, lines), lines), :]

    def users(g):
        return pl.ds(pl.multiple_of(g * UG, UG), UG)

    def by_interest(value):
        return [value[k * UG : (k + 1) * UG] for k in range(interests)]

    def gathered(ref, g):
        return jnp.concatenate([ref[k, users(g), :] for k in range(interests)], axis=0).astype(BF16)

    def put_pooled(g, value):
        for k, part in enumerate(by_interest(value)):
            pooled[k, users(g), :] = part

    def mask_of(g):
        owner = lax.broadcasted_iota(jnp.int32, (UG, width), 0)
        lane = lax.broadcasted_iota(jnp.int32, (UG, width), 1)
        alive = jnp.broadcast_to(live[pl.ds(g, 1), :], (UG, width))
        return (lane // LP == owner) & (alive > 0.0)

    def coupling(value, g):
        powers = [jnp.exp(part) for part in by_interest(value)]
        scale = 1.0 / functools.reduce(jnp.add, powers)
        mask = mask_of(g)
        return jnp.concatenate([jnp.where(mask, p * scale, 0.0) for p in powers], axis=0)

    def coupling_grad(weights, dots):
        ws, ds = by_interest(weights), by_interest(dots)
        inner = functools.reduce(jnp.add, [w * d for w, d in zip(ws, ds)])
        return jnp.concatenate([w * (d - inner) for w, d in zip(ws, ds)], axis=0)

    def loop(count, body):
        lax.fori_loop(0, count, lambda i, c: (body(i), c)[1], 0)

    def over_groups(stages, unroll=2):
        def body(i):
            ids = [i * unroll + j for j in range(unroll)]
            held = [() for _ in ids]
            for stage_fn in stages:
                held = [stage_fn(g, *h) for g, h in zip(ids, held)]

        loop(groups // unroll, body)

    def mapping(k):
        return bilinear[:, k * feature : (k + 1) * feature]

    def squash(summed):
        size = jnp.sum(summed * summed, axis=1, keepdims=True)
        root = jnp.sqrt(size + EPS)
        return size, root, root / (1.0 + size)

    def forward(keep, out):
        for k in range(interests):
            summed = jnp.dot(pooled[k].astype(BF16), mapping(k), preferred_element_type=F32)
            keep[k] = summed
            _, _, factor = squash(summed)
            out[k] = nt((summed * factor).astype(BF16), mapping(k))

    def squash_grad(summed, given):
        size, root, factor = squash(summed)
        along = jnp.sum(summed * given, axis=1, keepdims=True)
        above = 1.0 + size
        slope = 1.0 / (root * above) - 2.0 * root / (above * above)
        return given * factor + summed * (slope * along), factor

    def backward(keep, out):
        for k in range(interests):
            given = jnp.dot(pooled[k].astype(BF16), mapping(k), preferred_element_type=F32)
            grad, _ = squash_grad(keep[k], given)
            out[k] = nt(grad.astype(BF16), mapping(k))

    split_dense = 1024

    def widen(c):
        at = pl.ds(pl.multiple_of(c * split_dense, split_dense), split_dense)
        wide[at, :] = fetched[at, :].astype(F32)

    loop(fetched.shape[0] // split_dense, widen)
    stage[...] = jnp.zeros_like(stage)

    def first(g):
        for u in range(UG):
            for l in range(hist_len):
                slot = slots[g * (UG * hist_len) + u * hist_len + l]
                stage[pl.ds(2 * (u * LP + l), 2), :] = wide[two(slot), :]
        at = pl.ds(pl.multiple_of(g * width, width), width)
        for h in range(2):
            rows[at, h * HALF : (h + 1) * HALF] = stage[pl.ds(h, width, stride=2), :].astype(BF16)
        start = jnp.concatenate(
            [
                jnp.broadcast_to(first_logits[pl.ds(g * interests + k, 1), :], (UG, width))
                for k in range(interests)
            ],
            axis=0,
        )
        lanes(logits, g)[...] = start
        weights = coupling(start, g)
        lanes(w0, g)[...] = weights
        put_pooled(g, jnp.dot(weights.astype(BF16), block(g), preferred_element_type=F32))

    loop(groups, first)
    forward(s0, q0)

    def turn(q, w, last):
        def agree(g):
            return (nt(gathered(q, g), block(g)),)

        def reweigh(g, scores):
            value = lanes(logits, g)[...] + scores
            if not last:
                lanes(logits, g)[...] = value
            weights = coupling(value, g)
            lanes(w, g)[...] = weights
            return (weights.astype(BF16),)

        def pool(g, weights):
            put_pooled(g, jnp.dot(weights, block(g), preferred_element_type=F32))
            return ()

        over_groups([agree, reweigh, pool])

    turn(q0, w1, False)
    forward(s1, q1)
    turn(q1, w2, True)

    for k in range(interests):
        summed = jnp.dot(pooled[k].astype(BF16), mapping(k), preferred_element_type=F32)
        grad, factor = squash_grad(summed, cotangent[k])
        capsules[k] = (summed * factor).astype(BF16)
        g2[k] = nt(grad.astype(BF16), mapping(k))

    def turn_back(gr, w, z, add):
        def dots(g):
            return (nt(gathered(gr, g), block(g)),)

        def reweigh(g, value):
            grad = coupling_grad(lanes(w, g)[...], value)
            if add:
                grad = grad + lanes(logits, g)[...]
            else:
                lanes(logits, g)[...] = grad
            grad = grad.astype(BF16)
            lanes(z, g)[...] = grad
            return (grad,)

        def pool(g, grad):
            put_pooled(g, jnp.dot(grad, block(g), preferred_element_type=F32))
            return ()

        over_groups([dots, reweigh, pool])

    turn_back(g2, w2, z1, False)
    backward(s1, g1)
    turn_back(g1, w1, z0, True)
    backward(s0, g0)

    def copy_same(g):
        slot = lax.rem(g, 2)
        return pltpu.make_async_copy(
            same.at[pl.ds(pl.multiple_of(g * width, width), width), :],
            same_buf.at[slot],
            same_sem.at[slot],
        )

    copy_same(0).start()

    def clear(c):
        at = pl.ds(pl.multiple_of(c * split_dense, split_dense), split_dense)
        wide[at, :] = jnp.zeros((split_dense, HALF), F32)

    loop(fetched.shape[0] // split_dense, clear)

    def last(g):
        coefs = jnp.concatenate(
            [lanes(w, g)[...].astype(BF16) for w in (w0, w1, w2)]
            + [lanes(z, g)[...] for z in (z0, z1)],
            axis=0,
        )
        basis = jnp.concatenate([gathered(b, g) for b in (g0, g1, g2, q0, q1)], axis=0)
        grads = tn(coefs, basis).astype(BF16)

        @pl.when(g + 1 < groups)
        def _():
            copy_same(g + 1).start()

        copy_same(g).wait()
        part = width // 2
        for p in range(2):
            merged = jnp.dot(
                same_buf[lax.rem(g, 2), p * part : (p + 1) * part, :],
                grads[p * part : (p + 1) * part],
                preferred_element_type=F32,
            )
            for h in range(2):
                stage[pl.ds(2 * p * part + h, part, stride=2), :] = merged[:, h * HALF : (h + 1) * HALF]
        batch = hist_len // 2
        for u in range(UG):
            for b in range(2):
                ls = range(b * batch, (b + 1) * batch)
                at = [two(slots[g * (UG * hist_len) + u * hist_len + l]) for l in ls]
                held = [wide[a, :] for a in at]
                for a, value, l in zip(at, held, ls):
                    wide[a, :] = value + stage[pl.ds(2 * (u * LP + l), 2), :]

    loop(groups, last)

    def emit(c):
        at = pl.ds(pl.multiple_of(c * split_dense, split_dense), split_dense)
        slot_grads[at, :] = wide[at, :].astype(BF16)

    loop(fetched.shape[0] // split_dense, emit)


def route(slots, fetched, bilinear, lengths, init_logits, interest_grad):
    users_here, hist_len, interests = init_logits.shape
    feature = bilinear.shape[0]
    groups = users_here // UG
    width = UG * LP
    pad = LP - hist_len
    ids = jnp.pad(slots, ((0, 0), (0, pad)), constant_values=-1).reshape(users_here // 4, 4 * LP)
    place = jnp.arange(4 * LP, dtype=jnp.int32)
    batch = place // LP * 2 + (place % LP >= hist_len // 2)
    same = (ids[:, :, None] == ids[:, None, :]) & (batch[:, None] == batch[None, :])
    same = same.astype(BF16).reshape(users_here * LP, 4 * LP)
    live = (jnp.arange(LP, dtype=jnp.int32)[None, :] < lengths[:, None]).astype(F32)
    live = live.reshape(groups, width)
    first_logits = jnp.pad(jnp.transpose(init_logits, (0, 2, 1)), ((0, 0), (0, 0), (0, pad)))
    first_logits = first_logits.reshape(groups, UG, interests, LP)
    first_logits = jnp.transpose(first_logits, (0, 2, 1, 3)).reshape(groups * interests, width)
    cotangent = jnp.transpose(interest_grad, (1, 0, 2))
    lines = groups * interests * UG
    per_user = pltpu.VMEM((interests, users_here, feature), F32)
    capsules, slot_grads = pl.pallas_call(
        functools.partial(route_kernel, interests, hist_len),
        name="route_users",
        out_shape=(
            jax.ShapeDtypeStruct((interests, users_here, feature), BF16),
            jax.ShapeDtypeStruct(fetched.shape, BF16),
        ),
        in_specs=[smem()] + [vmem()] * 5 + [pl.BlockSpec(memory_space=pl.ANY)],
        out_specs=(vmem(), vmem()),
        scratch_shapes=[
            pltpu.VMEM(fetched.shape, F32),
            pltpu.VMEM((users_here * LP, feature), BF16),
            pltpu.VMEM((2 * width, HALF), F32),
        ]
        + [pltpu.VMEM((lines, width), F32)] * 4
        + [pltpu.VMEM((lines, width), BF16)] * 2
        + [per_user] * 9
        + [pltpu.VMEM((2, width, 4 * LP), BF16), pltpu.SemaphoreType.DMA((2,))],
        compiler_params=pltpu.CompilerParams(vmem_limit_bytes=60 * MIB),
    )(slots.reshape(-1), fetched, bilinear, first_logits, live, cotangent, same)
    return jnp.transpose(capsules, (1, 0, 2)), slot_grads


def local(item_table, bilinear, requests, history, lengths, init_logits, interest_grad):
    asked = requests[0]
    owners, slots = asked.shape
    table_rows = item_table.shape[0]

    def exchange(value):
        return lax.all_to_all(value, ("gx", "gy"), split_axis=0, concat_axis=0, tiled=True)

    wanted = exchange(asked).reshape(-1)
    found = fetch_rows(jnp.maximum(wanted, 0), item_table, slots)
    fetched = exchange(found)
    capsules, slot_grads = route(history, fetched, bilinear, lengths, init_logits, interest_grad)
    returned = exchange(slot_grads)
    targets = jnp.where(wanted >= 0, wanted, table_rows)
    return capsules, return_rows(targets, returned, table_rows, slots)


def solution(mesh):
    both = ("gx", "gy")
    placed = (
        P(both, None),
        P(),
        P(both, None, None),
        P(both, None),
        P(both),
        P(both, None, None),
        P(both, None, None),
    )
    return jax.shard_map(
        local,
        mesh=mesh,
        in_specs=placed,
        out_specs=(P(both, None, None), P(both, None)),
        check_vma=False,
    )
```

```python
import functools

import jax
import jax.numpy as jnp
from jax import lax
from jax.experimental import pallas as pl
from jax.experimental.pallas import tpu as pltpu
from jax.sharding import PartitionSpec as P

ITERS = 3
EPS = 1e-06
LP = 64
UG = 8
BATCH = 5
HALF = 128
MIB = 1024 * 1024
F32 = jnp.float32
BF16 = jnp.bfloat16


def vmem():
    return pl.BlockSpec(memory_space=pltpu.VMEM)


def smem():
    return pl.BlockSpec(memory_space=pltpu.SMEM)


def two(i):
    return pl.ds(pl.multiple_of(i, 2), 2)


def split_rows(src, dst, rows, step=512):
    def body(c, carry):
        at = pl.multiple_of(c * step, step)
        for h in range(2):
            dst[pl.ds(2 * at + h, step, stride=2), :] = src[
                pl.ds(at, step), h * HALF : (h + 1) * HALF
            ].astype(F32)
        return carry

    lax.fori_loop(0, rows // step, body, 0)


def fetch_kernel(slots, ids, table, out, wide, stage):
    rows = table.shape[0]
    lists = ids.shape[0] // slots
    split_rows(table, wide, rows)

    def body(c, carry):
        for j in range(slots):
            stage[pl.ds(2 * j, 2), :] = wide[two(ids.at[pl.ds(j * lists, lists)][c]), :]
        out[pl.ds(pl.multiple_of(c * 2 * slots, 2 * slots), 2 * slots), :] = stage[...].astype(BF16)
        return carry

    lax.fori_loop(0, lists, body, 0)


def fetch_rows(ids, table, slots):
    rows = table.shape[0]
    return pl.pallas_call(
        functools.partial(fetch_kernel, slots),
        name="fetch_rows",
        out_shape=jax.ShapeDtypeStruct((2 * ids.shape[0], HALF), BF16),
        in_specs=[smem(), vmem()],
        out_specs=vmem(),
        scratch_shapes=[pltpu.VMEM((2 * rows, HALF), F32), pltpu.VMEM((2 * slots, HALF), F32)],
        compiler_params=pltpu.CompilerParams(vmem_limit_bytes=40 * MIB),
    )(2 * ids.reshape(-1, slots).T.reshape(-1), table)


def add_lines(totals, count, batch, line_of, value_of):
    def load(n):
        lines = [line_of(n * batch + j) for j in range(batch)]
        return [(at, totals[n % 2][at, :]) for at in lines]

    held = load(0)
    for n in range(count // batch):
        later = load(n + 1) if (n + 1) * batch < count else None
        for j, (at, old) in enumerate(held):
            totals[n % 2][at, :] = old + value_of(n * batch + j)
        held = later


def return_kernel(slots, feed, ids, grads, out, total0, total1, stage):
    step = pl.program_id(0)
    chunk = grads.shape[0]
    totals = (total0, total1)
    lists = ids.shape[0] // slots
    part = lists // feed
    batch = 8

    @pl.when(step == 0)
    def _():
        def clear(c, carry):
            at = pl.ds(pl.multiple_of(c * 512, 512), 512)
            for total in totals:
                total[at, :] = jnp.zeros((512, HALF), F32)
            return carry

        lax.fori_loop(0, (total0.shape[0] - 16) // 512, clear, 0)

    @pl.when(step < feed)
    def _():
        stage[...] = grads[...].astype(F32)

        def body(c, carry):
            given = stage.at[pl.ds(pl.multiple_of(c * 2 * slots, 2 * slots), 2 * slots), :]

            add_lines(
                totals,
                slots,
                batch,
                lambda j: two(ids.at[pl.ds(j * lists, lists)][step * part + c]),
                lambda j: given[pl.ds(2 * j, 2), :],
            )
            return carry

        lax.fori_loop(0, part, body, 0)

    @pl.when(step >= feed)
    def _():
        rows = out.shape[0]
        at = pl.multiple_of((step - feed) * 2 * rows, 2 * rows)
        for h in range(2):
            lines = pl.ds(at + h, rows, stride=2)
            out[:, h * HALF : (h + 1) * HALF] = total0[lines, :] + total1[lines, :]


def return_rows(ids, grads, rows, slots):
    feed = 8
    drain = 8
    chunk = grads.shape[0] // feed
    return pl.pallas_call(
        functools.partial(return_kernel, slots, feed),
        name="return_rows",
        grid=(feed + drain,),
        out_shape=jax.ShapeDtypeStruct((rows, 2 * HALF), F32),
        in_specs=[smem(), pl.BlockSpec((chunk, HALF), lambda i: (jnp.minimum(i, feed - 1), 0))],
        out_specs=pl.BlockSpec((rows // drain, 2 * HALF), lambda i: (jnp.maximum(i - feed, 0), 0)),
        scratch_shapes=[pltpu.VMEM((2 * rows + 16, HALF), F32)] * 2 + [pltpu.VMEM((chunk, HALF), F32)],
        compiler_params=pltpu.CompilerParams(vmem_limit_bytes=40 * MIB),
    )(2 * ids.reshape(-1, slots).T.reshape(-1), grads)


def route_kernel(
    interests, hist_len,
    slots, fetched, bilinear, first_logits, live, cotangent, same,
    capsules, slot_grads,
    wide, more, rows, stage_a, stage_b, logits, w0, w1, w2, z0, z1, pooled, q0, q1, g0, g1, g2, s0, s1, s2,
    same_buf, same_sem,
):
    groups = live.shape[0]
    width = UG * LP
    lines = interests * UG
    feature = rows.shape[1]

    def nt(a, b):
        return lax.dot_general(a, b, (((1,), (1,)), ((), ())), preferred_element_type=F32)

    def tn(a, b):
        return lax.dot_general(a, b, (((0,), (0,)), ((), ())), preferred_element_type=F32)

    def block(g):
        return rows[pl.ds(pl.multiple_of(g * width, width), width), :]

    def lanes(ref, g):
        return ref.at[pl.ds(pl.multiple_of(g * lines, lines), lines), :]

    def users(g):
        return pl.ds(pl.multiple_of(g * UG, UG), UG)

    def by_interest(value):
        return [value[k * UG : (k + 1) * UG] for k in range(interests)]

    def gathered(ref, g):
        return jnp.concatenate([ref[k, users(g), :] for k in range(interests)], axis=0).astype(BF16)

    def put_pooled(g, value):
        for k, part in enumerate(by_interest(value)):
            pooled[k, users(g), :] = part

    def mask_of(g):
        owner = lax.broadcasted_iota(jnp.int32, (UG, width), 0)
        lane = lax.broadcasted_iota(jnp.int32, (UG, width), 1)
        alive = jnp.broadcast_to(live[pl.ds(g, 1), :], (UG, width))
        return (lane // LP == owner) & (alive > 0.0)

    def coupling(value, g):
        powers = [jnp.exp(part) for part in by_interest(value)]
        scale = 1.0 / functools.reduce(jnp.add, powers)
        mask = mask_of(g)
        return jnp.concatenate([jnp.where(mask, p * scale, 0.0) for p in powers], axis=0)

    def coupling_grad(weights, dots):
        ws, ds = by_interest(weights), by_interest(dots)
        inner = functools.reduce(jnp.add, [w * d for w, d in zip(ws, ds)])
        return jnp.concatenate([w * (d - inner) for w, d in zip(ws, ds)], axis=0)

    def loop(count, body):
        lax.fori_loop(0, count, lambda i, c: (body(i), c)[1], 0)

    def over_groups(stages, unroll=8):
        def body(i):
            ids = [i * unroll + j for j in range(unroll)]
            held = [() for _ in ids]
            for stage_fn in stages:
                held = [stage_fn(g, *h) for g, h in zip(ids, held)]

        loop(groups // unroll, body)

    def mapping(k):
        return bilinear[:, k * feature : (k + 1) * feature]

    def squash(summed):
        size = jnp.sum(summed * summed, axis=1, keepdims=True)
        root = jnp.sqrt(size + EPS)
        return size, root, root / (1.0 + size)

    def forward(keep, out):
        for k in range(interests):
            summed = jnp.dot(pooled[k].astype(BF16), mapping(k), preferred_element_type=F32)
            keep[k] = summed
            _, _, factor = squash(summed)
            out[k] = nt((summed * factor).astype(BF16), mapping(k))

    def squash_grad(summed, given):
        size, root, factor = squash(summed)
        along = jnp.sum(summed * given, axis=1, keepdims=True)
        above = 1.0 + size
        slope = 1.0 / (root * above) - 2.0 * root / (above * above)
        return given * factor + summed * (slope * along), factor

    def backward(keep, out):
        for k in range(interests):
            given = jnp.dot(pooled[k].astype(BF16), mapping(k), preferred_element_type=F32)
            grad, _ = squash_grad(keep[k], given)
            out[k] = nt(grad.astype(BF16), mapping(k))

    split_dense = 1024

    def widen(c):
        at = pl.ds(pl.multiple_of(c * split_dense, split_dense), split_dense)
        wide[at, :] = fetched[at, :].astype(F32)

    loop(fetched.shape[0] // split_dense, widen)
    for stage in (stage_a, stage_b):
        stage[...] = jnp.zeros_like(stage)

    def line_of(g, j):
        return two(slots.at[pl.ds(j * groups, groups)][g])

    def place(j):
        return pl.ds(2 * (j // hist_len * LP + j % hist_len), 2)

    behaviors = UG * hist_len

    def gather(g, stage):
        for j in range(behaviors):
            stage[place(j), :] = wide[line_of(g, j), :]

    def first(g, stage):
        at = pl.ds(pl.multiple_of(g * width, width), width)
        dense = jnp.concatenate(
            [stage[pl.ds(h, width, stride=2), :].astype(BF16) for h in range(2)], axis=1
        )
        rows[at, :] = dense
        start = jnp.concatenate(
            [
                jnp.broadcast_to(first_logits[pl.ds(g * interests + k, 1), :], (UG, width))
                for k in range(interests)
            ],
            axis=0,
        )
        lanes(logits, g)[...] = start
        weights = coupling(start, g)
        lanes(w0, g)[...] = weights
        put_pooled(g, jnp.dot(weights.astype(BF16), dense, preferred_element_type=F32))

    gather(0, stage_a)

    def first_pair(i):
        gather(2 * i + 1, stage_b)
        first(2 * i, stage_a)
        gather(jnp.minimum(2 * i + 2, groups - 1), stage_a)
        first(2 * i + 1, stage_b)

    loop(groups // 2, first_pair)
    forward(s0, q0)

    def turn(q, w, last):
        def agree(g):
            return (nt(gathered(q, g), block(g)),)

        def reweigh(g, scores):
            value = lanes(logits, g)[...] + scores
            if not last:
                lanes(logits, g)[...] = value
            weights = coupling(value, g)
            lanes(w, g)[...] = weights
            return (weights.astype(BF16),)

        def pool(g, weights):
            put_pooled(g, jnp.dot(weights, block(g), preferred_element_type=F32))
            return ()

        over_groups([agree, reweigh, pool])

    turn(q0, w1, False)
    forward(s1, q1)
    turn(q1, w2, True)

    for k in range(interests):
        summed = jnp.dot(pooled[k].astype(BF16), mapping(k), preferred_element_type=F32)
        grad, factor = squash_grad(summed, cotangent[k])
        capsules[k] = (summed * factor).astype(BF16)
        g2[k] = nt(grad.astype(BF16), mapping(k))

    def turn_back(gr, w, z, add):
        def dots(g):
            return (nt(gathered(gr, g), block(g)),)

        def reweigh(g, value):
            grad = coupling_grad(lanes(w, g)[...], value)
            if add:
                grad = grad + lanes(logits, g)[...]
            else:
                lanes(logits, g)[...] = grad
            grad = grad.astype(BF16)
            lanes(z, g)[...] = grad
            return (grad,)

        def pool(g, grad):
            put_pooled(g, jnp.dot(grad, block(g), preferred_element_type=F32))
            return ()

        over_groups([dots, reweigh, pool])

    turn_back(g2, w2, z1, False)
    backward(s1, g1)
    turn_back(g1, w1, z0, True)
    backward(s0, g0)

    pairs = groups // 2

    def copy_same(i):
        slot = lax.rem(i, 2)
        return pltpu.make_async_copy(
            same.at[pl.ds(pl.multiple_of((2 * i + 1) * width, width), 2 * width), :],
            same_buf.at[slot],
            same_sem.at[slot],
        )

    head = pltpu.make_async_copy(
        same.at[pl.ds(0, width), :], same_buf.at[1, pl.ds(0, width), :], same_sem.at[1]
    )
    head.start()
    copy_same(0).start()

    def clear(c):
        at = pl.ds(pl.multiple_of(c * split_dense, split_dense), split_dense)
        for total in (wide, more):
            total[at, :] = jnp.zeros((split_dense, HALF), F32)

    loop(fetched.shape[0] // split_dense, clear)

    def spread(g, equal, stage):
        coefs = jnp.concatenate(
            [lanes(w, g)[...].astype(BF16) for w in (w0, w1, w2)]
            + [lanes(z, g)[...] for z in (z0, z1)],
            axis=0,
        )
        basis = jnp.concatenate([gathered(b, g) for b in (g0, g1, g2, q0, q1)], axis=0)
        grads = tn(coefs, basis).astype(BF16)
        part = width // 2
        for p in range(2):
            merged = jnp.dot(
                equal[p * part : (p + 1) * part, :],
                grads[p * part : (p + 1) * part],
                preferred_element_type=F32,
            )
            for h in range(2):
                stage[pl.ds(2 * p * part + h, part, stride=2), :] = merged[:, h * HALF : (h + 1) * HALF]

    def scatter(g, stage):
        add_lines(
            (wide, more),
            behaviors,
            BATCH,
            lambda j: line_of(g, j),
            lambda j: stage[place(j), :],
        )

    head.wait()
    spread(0, same_buf.at[1, pl.ds(0, width), :], stage_a)

    def last_pair(i):
        copy_same(i).wait()

        @pl.when(i + 1 < pairs)
        def _():
            copy_same(i + 1).start()

        equal = same_buf.at[lax.rem(i, 2)]
        scatter(2 * i, stage_a)
        spread(2 * i + 1, equal.at[pl.ds(0, width), :], stage_b)
        scatter(2 * i + 1, stage_b)
        spread(jnp.minimum(2 * i + 2, groups - 1), equal.at[pl.ds(width, width), :], stage_a)

    loop(pairs, last_pair)

    def emit(c):
        at = pl.ds(pl.multiple_of(c * split_dense, split_dense), split_dense)
        slot_grads[at, :] = (wide[at, :] + more[at, :]).astype(BF16)

    loop(fetched.shape[0] // split_dense, emit)


def route(slots, fetched, bilinear, lengths, init_logits, interest_grad):
    users_here, hist_len, interests = init_logits.shape
    feature = bilinear.shape[0]
    groups = users_here // UG
    width = UG * LP
    pad = LP - hist_len
    ids = jnp.pad(slots, ((0, UG), (0, pad)), constant_values=-1).reshape(-1, 4 * LP)
    place = jnp.arange(4 * LP, dtype=jnp.int32)
    batch = place // LP * LP + place % LP // BATCH
    same = (ids[:, :, None] == ids[:, None, :]) & (batch[:, None] == batch[None, :])
    same = same.astype(BF16).reshape(-1, 4 * LP)
    live = (jnp.arange(LP, dtype=jnp.int32)[None, :] < lengths[:, None]).astype(F32)
    live = live.reshape(groups, width)
    first_logits = jnp.pad(jnp.transpose(init_logits, (0, 2, 1)), ((0, 0), (0, 0), (0, pad)))
    first_logits = first_logits.reshape(groups, UG, interests, LP)
    first_logits = jnp.transpose(first_logits, (0, 2, 1, 3)).reshape(groups * interests, width)
    cotangent = jnp.transpose(interest_grad, (1, 0, 2))
    lines = groups * interests * UG
    lines_of = (2 * slots).reshape(groups, UG * hist_len).T.reshape(-1)
    per_user = pltpu.VMEM((interests, users_here, feature), F32)
    capsules, slot_grads = pl.pallas_call(
        functools.partial(route_kernel, interests, hist_len),
        name="route_users",
        out_shape=(
            jax.ShapeDtypeStruct((interests, users_here, feature), BF16),
            jax.ShapeDtypeStruct(fetched.shape, BF16),
        ),
        in_specs=[smem()] + [vmem()] * 5 + [pl.BlockSpec(memory_space=pl.ANY)],
        out_specs=(vmem(), vmem()),
        scratch_shapes=[
            pltpu.VMEM(fetched.shape, F32),
            pltpu.VMEM(fetched.shape, F32),
            pltpu.VMEM((users_here * LP, feature), BF16),
            pltpu.VMEM((2 * width, HALF), F32),
            pltpu.VMEM((2 * width, HALF), F32),
        ]
        + [pltpu.VMEM((lines, width), F32)] * 4
        + [pltpu.VMEM((lines, width), BF16)] * 2
        + [per_user] * 9
        + [pltpu.VMEM((2, 2 * width, 4 * LP), BF16), pltpu.SemaphoreType.DMA((2,))],
        compiler_params=pltpu.CompilerParams(vmem_limit_bytes=60 * MIB),
    )(lines_of, fetched, bilinear, first_logits, live, cotangent, same)
    return jnp.transpose(capsules, (1, 0, 2)), slot_grads


def local(item_table, bilinear, requests, history, lengths, init_logits, interest_grad):
    asked = requests[0]
    owners, slots = asked.shape
    table_rows = item_table.shape[0]

    def exchange(value):
        return lax.all_to_all(value, ("gx", "gy"), split_axis=0, concat_axis=0, tiled=True)

    wanted = exchange(asked).reshape(-1)
    found = fetch_rows(jnp.maximum(wanted, 0), item_table, slots)
    fetched = exchange(found)
    capsules, slot_grads = route(history, fetched, bilinear, lengths, init_logits, interest_grad)
    returned = exchange(slot_grads)
    targets = jnp.where(wanted >= 0, wanted, table_rows)
    return capsules, return_rows(targets, returned, table_rows, slots)


def solution(mesh):
    both = ("gx", "gy")
    placed = (
        P(both, None),
        P(),
        P(both, None, None),
        P(both, None),
        P(both),
        P(both, None, None),
        P(both, None, None),
    )
    return jax.shard_map(
        local,
        mesh=mesh,
        in_specs=placed,
        out_specs=(P(both, None, None), P(both, None)),
        check_vma=False,
    )
```

```python
import functools

import jax
import jax.numpy as jnp
from jax import lax
from jax.experimental import pallas as pl
from jax.experimental.pallas import tpu as pltpu
from jax.sharding import PartitionSpec as P

ITERS = 3
EPS = 1e-06
LP = 64
UG = 8
BATCH = 5
HALF = 128
MIB = 1024 * 1024
F32 = jnp.float32
BF16 = jnp.bfloat16
MESH = pl.DeviceIdType.MESH


def vmem():
    return pl.BlockSpec(memory_space=pltpu.VMEM)


def smem():
    return pl.BlockSpec(memory_space=pltpu.SMEM)


def two(i):
    return pl.ds(pl.multiple_of(i, 2), 2)


def peer(step, sizes):
    a, b, c, d = step % 4, step // 4 % 4, step // 16 % 4, step // 64
    gx, gy = lax.axis_index("gx"), lax.axis_index("gy")
    z = (gx // 2 + a + b) % 4
    core = (gx + a // 2 + d) % 2
    y = (gy // 4 + a + b + c) % 4
    x = (gy + a) % 4
    return z * 2 + core, y * 4 + x


def greet(sizes):
    barrier = pltpu.get_barrier_semaphore()

    def body(step, carry):
        pl.semaphore_signal(barrier, inc=1, device_id=peer(step, sizes), device_id_type=MESH)
        return carry

    lax.fori_loop(1, sizes[0] * sizes[1], body, 0)
    return barrier


def send(step, sizes, source, target, send_sem, recv_sem):
    gx, gy = peer(step, sizes)
    me = lax.axis_index("gx") * sizes[1] + lax.axis_index("gy")
    pltpu.make_async_remote_copy(
        src_ref=source.at[gx * sizes[1] + gy],
        dst_ref=target.at[me],
        send_sem=send_sem,
        recv_sem=recv_sem,
        device_id=(gx, gy),
        device_id_type=MESH,
    ).start()


def all_but_one(ref, sem):
    part = ref.at[pl.ds(0, ref.shape[0] - 1)]
    pltpu.make_async_copy(part, part, sem).wait()


def fetch_kernel(
    sizes, slots, asked, table, fetched, wanted,
    narrow, wide, stage, found, ids, table_sem, own_sem, ids_sem, sems,
):
    owners = sizes[0] * sizes[1]
    rows = table.shape[0]
    me = lax.axis_index("gx") * sizes[1] + lax.axis_index("gy")
    fill = pltpu.make_async_copy(table, narrow, table_sem)
    fill.start()
    own = pltpu.make_async_copy(asked.at[me], wanted.at[me], own_sem)
    own.start()
    barrier = greet(sizes)
    fill.wait()

    def widen(c, carry):
        at = pl.ds(pl.multiple_of(c * 512, 512), 512)
        for h in range(2):
            wide[at, h, :] = narrow[at, h * HALF : (h + 1) * HALF].astype(F32)
        return carry

    early = rows // 512 * 5 // 8
    lax.fori_loop(0, early, widen, 0)
    pl.semaphore_wait(barrier, owners - 1)

    def ask(step, carry):
        send(step, sizes, asked, wanted, sems.at[0], sems.at[1])
        return carry

    lax.fori_loop(1, owners, ask, 0)
    lax.fori_loop(early, rows // 512, widen, 0)
    wide[rows] = jnp.zeros((2, HALF), F32)
    own.wait()
    all_but_one(asked, sems.at[0])
    all_but_one(wanted, sems.at[1])
    load = pltpu.make_async_copy(wanted, ids, ids_sem)
    load.start()
    load.wait()

    def gather(block):
        for j in range(slots):
            stage[pl.ds(2 * j, 2), :] = wide[ids[block, 0, j]]
        found[block] = stage[...].astype(BF16)

    gather(me)
    keep = pltpu.make_async_copy(found.at[me], fetched.at[me], own_sem)

    def serve(step, carry):
        gx, gy = peer(step, sizes)
        gather(gx * sizes[1] + gy)

        @pl.when(step > 1)
        def _():
            send(step - 1, sizes, found, fetched, sems.at[2], sems.at[3])

        return carry

    lax.fori_loop(1, owners, serve, 0)
    keep.start()
    send(owners - 1, sizes, found, fetched, sems.at[2], sems.at[3])
    keep.wait()
    all_but_one(found, sems.at[2])
    all_but_one(fetched, sems.at[3])


def fetch_rows(asked, table, sizes, slots):
    rows, feature = table.shape
    owners = asked.shape[0]
    hbm = pl.BlockSpec(memory_space=pl.ANY)
    return pl.pallas_call(
        functools.partial(fetch_kernel, sizes, slots),
        name="fetch_rows",
        out_shape=(
            jax.ShapeDtypeStruct((owners, 2 * slots, HALF), BF16),
            jax.ShapeDtypeStruct(asked.shape, jnp.int32),
        ),
        in_specs=[vmem(), hbm],
        out_specs=(hbm, vmem()),
        scratch_shapes=[
            pltpu.VMEM((rows, feature), BF16),
            pltpu.VMEM((rows + 4, 2, HALF), F32),
            pltpu.VMEM((2 * slots, HALF), F32),
            pltpu.VMEM((owners, 2 * slots, HALF), BF16),
            pltpu.SMEM(asked.shape, jnp.int32),
            pltpu.SemaphoreType.DMA,
            pltpu.SemaphoreType.DMA,
            pltpu.SemaphoreType.DMA,
            pltpu.SemaphoreType.DMA((4,)),
        ],
        compiler_params=pltpu.CompilerParams(
            collective_id=0, has_side_effects=True, vmem_limit_bytes=40 * MIB
        ),
    )(asked, table)


def exchange_kernel(sizes, given, taken, own_sem, sems):
    owners = sizes[0] * sizes[1]
    me = lax.axis_index("gx") * sizes[1] + lax.axis_index("gy")
    barrier = greet(sizes)
    own = pltpu.make_async_copy(given.at[me], taken.at[me], own_sem)
    own.start()
    pl.semaphore_wait(barrier, owners - 1)

    def serve(step, carry):
        send(step, sizes, given, taken, sems.at[0], sems.at[1])
        return carry

    lax.fori_loop(1, owners, serve, 0)
    own.wait()
    all_but_one(given, sems.at[0])
    all_but_one(taken, sems.at[1])


def exchange(value, sizes):
    hbm = pl.BlockSpec(memory_space=pl.ANY)
    return pl.pallas_call(
        functools.partial(exchange_kernel, sizes),
        name="exchange",
        out_shape=jax.ShapeDtypeStruct(value.shape, value.dtype),
        in_specs=[hbm],
        out_specs=hbm,
        scratch_shapes=[pltpu.SemaphoreType.DMA, pltpu.SemaphoreType.DMA((2,))],
        compiler_params=pltpu.CompilerParams(
            collective_id=1, has_side_effects=True, vmem_limit_bytes=40 * MIB
        ),
    )(value)


def add_lines(totals, count, batch, line_of, value_of):
    def load(n):
        lines = [line_of(n * batch + j) for j in range(batch)]
        return [(at, totals[n % 2][at, :]) for at in lines]

    held = load(0)
    for n in range(count // batch):
        later = load(n + 1) if (n + 1) * batch < count else None
        for j, (at, old) in enumerate(held):
            totals[n % 2][at, :] = old + value_of(n * batch + j)
        held = later


def return_kernel(slots, feed, ids, grads, out, total0, total1, stage):
    step = pl.program_id(0)
    chunk = grads.shape[0]
    totals = (total0, total1)
    lists = ids.shape[0] // slots
    part = lists // feed
    batch = 8

    @pl.when(step == 0)
    def _():
        def clear(c, carry):
            at = pl.ds(pl.multiple_of(c * 512, 512), 512)
            for total in totals:
                total[at, :] = jnp.zeros((512, HALF), F32)
            return carry

        lax.fori_loop(0, (total0.shape[0] - 16) // 512, clear, 0)

    @pl.when(step < feed)
    def _():
        stage[...] = grads[...].astype(F32)

        def body(c, carry):
            given = stage.at[pl.ds(pl.multiple_of(c * 2 * slots, 2 * slots), 2 * slots), :]

            add_lines(
                totals,
                slots,
                batch,
                lambda j: two(ids.at[pl.ds(j * lists, lists)][step * part + c]),
                lambda j: given[pl.ds(2 * j, 2), :],
            )
            return carry

        lax.fori_loop(0, part, body, 0)

    @pl.when(step >= feed)
    def _():
        rows = out.shape[0]
        at = pl.multiple_of((step - feed) * 2 * rows, 2 * rows)
        for h in range(2):
            lines = pl.ds(at + h, rows, stride=2)
            out[:, h * HALF : (h + 1) * HALF] = total0[lines, :] + total1[lines, :]


def return_rows(ids, grads, rows, slots):
    feed = 8
    drain = 8
    chunk = grads.shape[0] // feed
    return pl.pallas_call(
        functools.partial(return_kernel, slots, feed),
        name="return_rows",
        grid=(feed + drain,),
        out_shape=jax.ShapeDtypeStruct((rows, 2 * HALF), F32),
        in_specs=[smem(), pl.BlockSpec((chunk, HALF), lambda i: (jnp.minimum(i, feed - 1), 0))],
        out_specs=pl.BlockSpec((rows // drain, 2 * HALF), lambda i: (jnp.maximum(i - feed, 0), 0)),
        scratch_shapes=[pltpu.VMEM((2 * rows + 16, HALF), F32)] * 2 + [pltpu.VMEM((chunk, HALF), F32)],
        compiler_params=pltpu.CompilerParams(vmem_limit_bytes=40 * MIB),
    )(ids.T.reshape(-1), grads)


def route_kernel(
    interests, hist_len,
    slots, fetched, bilinear, first_logits, live, cotangent, keys,
    capsules, slot_grads,
    wide, more, rows, stage_a, stage_b, logits, w0, w1, w2, z0, z1, pooled, q0, q1, g0, g1, g2, s0, s1, s2,
):
    groups = live.shape[0]
    width = UG * LP
    lines = interests * UG
    feature = rows.shape[1]

    def nt(a, b):
        return lax.dot_general(a, b, (((1,), (1,)), ((), ())), preferred_element_type=F32)

    def tn(a, b):
        return lax.dot_general(a, b, (((0,), (0,)), ((), ())), preferred_element_type=F32)

    def block(g):
        return rows[pl.ds(pl.multiple_of(g * width, width), width), :]

    def lanes(ref, g):
        return ref.at[pl.ds(pl.multiple_of(g * lines, lines), lines), :]

    def users(g):
        return pl.ds(pl.multiple_of(g * UG, UG), UG)

    def by_interest(value):
        return [value[k * UG : (k + 1) * UG] for k in range(interests)]

    def gathered(ref, g):
        return jnp.concatenate([ref[k, users(g), :] for k in range(interests)], axis=0).astype(BF16)

    def put_pooled(g, value):
        for k, part in enumerate(by_interest(value)):
            pooled[k, users(g), :] = part

    def mask_of(g):
        owner = lax.broadcasted_iota(jnp.int32, (UG, width), 0)
        lane = lax.broadcasted_iota(jnp.int32, (UG, width), 1)
        alive = jnp.broadcast_to(live[pl.ds(g, 1), :], (UG, width))
        return (lane // LP == owner) & (alive > 0.0)

    def coupling(value, g):
        powers = [jnp.exp(part) for part in by_interest(value)]
        scale = 1.0 / functools.reduce(jnp.add, powers)
        mask = mask_of(g)
        return jnp.concatenate([jnp.where(mask, p * scale, 0.0) for p in powers], axis=0)

    def coupling_grad(weights, dots):
        ws, ds = by_interest(weights), by_interest(dots)
        inner = functools.reduce(jnp.add, [w * d for w, d in zip(ws, ds)])
        return jnp.concatenate([w * (d - inner) for w, d in zip(ws, ds)], axis=0)

    def loop(count, body):
        lax.fori_loop(0, count, lambda i, c: (body(i), c)[1], 0)

    def over_groups(stages, unroll=8):
        def body(i):
            ids = [i * unroll + j for j in range(unroll)]
            held = [() for _ in ids]
            for stage_fn in stages:
                held = [stage_fn(g, *h) for g, h in zip(ids, held)]

        loop(groups // unroll, body)

    def mapping(k):
        return bilinear[:, k * feature : (k + 1) * feature]

    def squash(summed):
        size = jnp.sum(summed * summed, axis=1, keepdims=True)
        root = jnp.sqrt(size + EPS)
        return size, root, root / (1.0 + size)

    def forward(keep, out):
        for k in range(interests):
            summed = jnp.dot(pooled[k].astype(BF16), mapping(k), preferred_element_type=F32)
            keep[k] = summed
            _, _, factor = squash(summed)
            out[k] = nt((summed * factor).astype(BF16), mapping(k))

    def squash_grad(summed, given):
        size, root, factor = squash(summed)
        along = jnp.sum(summed * given, axis=1, keepdims=True)
        above = 1.0 + size
        slope = 1.0 / (root * above) - 2.0 * root / (above * above)
        return given * factor + summed * (slope * along), factor

    def backward(keep, out):
        for k in range(interests):
            given = jnp.dot(pooled[k].astype(BF16), mapping(k), preferred_element_type=F32)
            grad, _ = squash_grad(keep[k], given)
            out[k] = nt(grad.astype(BF16), mapping(k))

    split_dense = 1024

    def widen(c):
        at = pl.ds(pl.multiple_of(c * split_dense, split_dense), split_dense)
        wide[at, :] = fetched[at, :].astype(F32)

    loop(fetched.shape[0] // split_dense, widen)
    for stage in (stage_a, stage_b):
        stage[...] = jnp.zeros_like(stage)

    def line_of(g, j):
        return two(slots.at[pl.ds(j * groups, groups)][g])

    def place(j):
        return pl.ds(2 * (j // hist_len * LP + j % hist_len), 2)

    behaviors = UG * hist_len

    def gather(g, stage):
        for j in range(behaviors):
            stage[place(j), :] = wide[line_of(g, j), :]

    def first(g, stage):
        at = pl.ds(pl.multiple_of(g * width, width), width)
        dense = jnp.concatenate(
            [stage[pl.ds(h, width, stride=2), :].astype(BF16) for h in range(2)], axis=1
        )
        rows[at, :] = dense
        start = jnp.concatenate(
            [
                jnp.broadcast_to(first_logits[pl.ds(g * interests + k, 1), :], (UG, width))
                for k in range(interests)
            ],
            axis=0,
        )
        lanes(logits, g)[...] = start
        weights = coupling(start, g)
        lanes(w0, g)[...] = weights
        put_pooled(g, jnp.dot(weights.astype(BF16), dense, preferred_element_type=F32))

    gather(0, stage_a)

    def first_pair(i):
        gather(2 * i + 1, stage_b)
        first(2 * i, stage_a)
        gather(jnp.minimum(2 * i + 2, groups - 1), stage_a)
        first(2 * i + 1, stage_b)

    loop(groups // 2, first_pair)
    forward(s0, q0)

    def turn(q, w, last):
        def agree(g):
            return (nt(gathered(q, g), block(g)),)

        def reweigh(g, scores):
            value = lanes(logits, g)[...] + scores
            if not last:
                lanes(logits, g)[...] = value
            weights = coupling(value, g)
            lanes(w, g)[...] = weights
            return (weights.astype(BF16),)

        def pool(g, weights):
            put_pooled(g, jnp.dot(weights, block(g), preferred_element_type=F32))
            return ()

        over_groups([agree, reweigh, pool])

    turn(q0, w1, False)
    forward(s1, q1)
    turn(q1, w2, True)

    for k in range(interests):
        summed = jnp.dot(pooled[k].astype(BF16), mapping(k), preferred_element_type=F32)
        grad, factor = squash_grad(summed, cotangent[k])
        capsules[k] = (summed * factor).astype(BF16)
        g2[k] = nt(grad.astype(BF16), mapping(k))

    def turn_back(gr, w, z, add):
        def dots(g):
            return (nt(gathered(gr, g), block(g)),)

        def reweigh(g, value):
            grad = coupling_grad(lanes(w, g)[...], value)
            if add:
                grad = grad + lanes(logits, g)[...]
            else:
                lanes(logits, g)[...] = grad
            grad = grad.astype(BF16)
            lanes(z, g)[...] = grad
            return (grad,)

        def pool(g, grad):
            put_pooled(g, jnp.dot(grad, block(g), preferred_element_type=F32))
            return ()

        over_groups([dots, reweigh, pool])

    turn_back(g2, w2, z1, False)
    backward(s1, g1)
    turn_back(g1, w1, z0, True)
    backward(s0, g0)

    def clear(c):
        at = pl.ds(pl.multiple_of(c * split_dense, split_dense), split_dense)
        for total in (wide, more):
            total[at, :] = jnp.zeros((split_dense, HALF), F32)

    loop(fetched.shape[0] // split_dense, clear)

    def spread(g, stage):
        coefs = jnp.concatenate(
            [lanes(w, g)[...].astype(BF16) for w in (w0, w1, w2)]
            + [lanes(z, g)[...] for z in (z0, z1)],
            axis=0,
        )
        basis = jnp.concatenate([gathered(b, g) for b in (g0, g1, g2, q0, q1)], axis=0)
        grads = tn(coefs, basis).astype(BF16)
        part = width // 2
        for p in range(2):
            key = keys[pl.ds(2 * g + p, 1), :]
            column = jnp.transpose(jnp.broadcast_to(key, (UG, part)))[:, :1]
            merged = jnp.dot(
                jnp.where(column == key, 1.0, 0.0).astype(BF16),
                grads[p * part : (p + 1) * part],
                preferred_element_type=F32,
            )
            for h in range(2):
                stage[pl.ds(2 * p * part + h, part, stride=2), :] = merged[:, h * HALF : (h + 1) * HALF]

    def scatter(g, stage):
        add_lines(
            (wide, more),
            behaviors,
            BATCH,
            lambda j: line_of(g, j),
            lambda j: stage[place(j), :],
        )

    spread(0, stage_a)

    def last_pair(i):
        scatter(2 * i, stage_a)
        spread(2 * i + 1, stage_b)
        scatter(2 * i + 1, stage_b)
        spread(jnp.minimum(2 * i + 2, groups - 1), stage_a)

    loop(groups // 2, last_pair)

    def emit(c):
        at = pl.ds(pl.multiple_of(c * split_dense, split_dense), split_dense)
        slot_grads[at, :] = (wide[at, :] + more[at, :]).astype(BF16)

    loop(fetched.shape[0] // split_dense, emit)


def route(slots, fetched, bilinear, lengths, init_logits, interest_grad):
    users_here, hist_len, interests = init_logits.shape
    feature = bilinear.shape[0]
    groups = users_here // UG
    width = UG * LP
    pad = LP - hist_len
    batch = jnp.arange(hist_len, dtype=jnp.int32) // BATCH + LP * (jnp.arange(users_here) % 4)[:, None]
    keys = (slots * (4 * LP) + batch).astype(F32)
    keys = jnp.pad(keys, ((0, 0), (0, pad)), constant_values=-1.0).reshape(-1, 4 * LP)
    live = (jnp.arange(LP, dtype=jnp.int32)[None, :] < lengths[:, None]).astype(F32)
    live = live.reshape(groups, width)
    first_logits = jnp.pad(jnp.transpose(init_logits, (0, 2, 1)), ((0, 0), (0, 0), (0, pad)))
    first_logits = first_logits.reshape(groups, UG, interests, LP)
    first_logits = jnp.transpose(first_logits, (0, 2, 1, 3)).reshape(groups * interests, width)
    cotangent = jnp.transpose(interest_grad, (1, 0, 2))
    lines = groups * interests * UG
    lines_of = (2 * slots).reshape(groups, UG * hist_len).T.reshape(-1)
    per_user = pltpu.VMEM((interests, users_here, feature), F32)
    capsules, slot_grads = pl.pallas_call(
        functools.partial(route_kernel, interests, hist_len),
        name="route_users",
        out_shape=(
            jax.ShapeDtypeStruct((interests, users_here, feature), BF16),
            jax.ShapeDtypeStruct(fetched.shape, BF16),
        ),
        in_specs=[smem()] + [vmem()] * 6,
        out_specs=(vmem(), vmem()),
        scratch_shapes=[
            pltpu.VMEM(fetched.shape, F32),
            pltpu.VMEM(fetched.shape, F32),
            pltpu.VMEM((users_here * LP, feature), BF16),
            pltpu.VMEM((2 * width, HALF), F32),
            pltpu.VMEM((2 * width, HALF), F32),
        ]
        + [pltpu.VMEM((lines, width), F32)] * 4
        + [pltpu.VMEM((lines, width), BF16)] * 2
        + [per_user] * 9,
        compiler_params=pltpu.CompilerParams(vmem_limit_bytes=60 * MIB),
    )(lines_of, fetched, bilinear, first_logits, live, cotangent, keys)
    return jnp.transpose(capsules, (1, 0, 2)), slot_grads


def local(sizes, item_table, bilinear, requests, history, lengths, init_logits, interest_grad):
    asked = requests[0]
    owners, slots = asked.shape
    table_rows = item_table.shape[0]
    asked = jnp.where(asked >= 0, asked, table_rows)
    asked = jnp.pad(asked, ((0, 0), (0, 128 - slots)))[:, None, :]
    fetched, wanted = fetch_rows(asked, item_table, sizes, slots)
    fetched = fetched.reshape(-1, HALF)
    capsules, slot_grads = route(history, fetched, bilinear, lengths, init_logits, interest_grad)
    returned = exchange(slot_grads.reshape(owners, 2 * slots, HALF), sizes).reshape(-1, HALF)
    return capsules, return_rows(2 * wanted[:, 0, :slots], returned, table_rows, slots)


def solution(mesh):
    both = ("gx", "gy")
    placed = (
        P(both, None),
        P(),
        P(both, None, None),
        P(both, None),
        P(both),
        P(both, None, None),
        P(both, None, None),
    )
    return jax.shard_map(
        functools.partial(local, (mesh.shape["gx"], mesh.shape["gy"])),
        mesh=mesh,
        in_specs=placed,
        out_specs=(P(both, None, None), P(both, None)),
        check_vma=False,
    )
```

```python
import functools

import jax
import jax.numpy as jnp
from jax import lax
from jax.experimental import pallas as pl
from jax.experimental.pallas import tpu as pltpu
from jax.sharding import PartitionSpec as P

ITERS = 3
EPS = 1e-06
LP = 64
UG = 8
BATCH = 5
HALF = 128
MIB = 1024 * 1024
F32 = jnp.float32
BF16 = jnp.bfloat16
MESH = pl.DeviceIdType.MESH


def vmem():
    return pl.BlockSpec(memory_space=pltpu.VMEM)


def smem():
    return pl.BlockSpec(memory_space=pltpu.SMEM)


def two(i):
    return pl.ds(pl.multiple_of(i, 2), 2)


def peer(step):
    a, b, c, d = step % 4, step // 4 % 4, step // 16 % 4, step // 64
    gx, gy = lax.axis_index("gx"), lax.axis_index("gy")
    z = (gx // 2 + a + b) % 4
    core = (gx + a // 2 + d) % 2
    y = (gy // 4 + a + b + c) % 4
    x = (gy + a) % 4
    return z * 2 + core, y * 4 + x


def partners():
    gx, gy = lax.axis_index("gx"), lax.axis_index("gy")
    z = [(gx // 2 + i) % 4 * 2 for i in range(4)]
    core = [(gx + i) % 2 for i in range(2)]
    y = [(gy // 4 + i) % 4 * 4 for i in range(4)]
    x = [(gy + i) % 4 for i in range(4)]
    found = []
    for step in range(1, 128):
        a, b, c, d = step % 4, step // 4 % 4, step // 16 % 4, step // 64
        found.append((z[(a + b) % 4] + core[(a // 2 + d) % 2], y[(a + b + c) % 4] + x[a]))
    return found


def greet(others):
    barrier = pltpu.get_barrier_semaphore()
    for other in others:
        pl.semaphore_signal(barrier, inc=1, device_id=other, device_id_type=MESH)
    return barrier


def send(other, sizes, source, target, send_sem, recv_sem):
    gx, gy = other
    me = lax.axis_index("gx") * sizes[1] + lax.axis_index("gy")
    pltpu.make_async_remote_copy(
        src_ref=source.at[gx * sizes[1] + gy],
        dst_ref=target.at[me],
        send_sem=send_sem,
        recv_sem=recv_sem,
        device_id=(gx, gy),
        device_id_type=MESH,
    ).start()


def all_but_one(ref, sem):
    part = ref.at[pl.ds(0, ref.shape[0] - 1)]
    pltpu.make_async_copy(part, part, sem).wait()


def fetch_kernel(
    sizes, slots, asked, table, fetched, wanted,
    narrow, wide, stage, found, ids, table_sem, own_sem, ids_sem, sems,
):
    owners = sizes[0] * sizes[1]
    rows = table.shape[0]
    me = lax.axis_index("gx") * sizes[1] + lax.axis_index("gy")
    fill = pltpu.make_async_copy(table, narrow, table_sem)
    fill.start()
    own = pltpu.make_async_copy(asked.at[me], wanted.at[me], own_sem)
    own.start()
    others = partners()
    barrier = greet(others)
    fill.wait()

    def widen(c, carry):
        at = pl.ds(pl.multiple_of(c * 512, 512), 512)
        for h in range(2):
            wide[at, h, :] = narrow[at, h * HALF : (h + 1) * HALF].astype(F32)
        return carry

    early = rows // 512 * 5 // 8
    lax.fori_loop(0, early, widen, 0)
    pl.semaphore_wait(barrier, owners - 1)

    for other in others:
        send(other, sizes, asked, wanted, sems.at[0], sems.at[1])
    lax.fori_loop(early, rows // 512, widen, 0)
    wide[rows] = jnp.zeros((2, HALF), F32)
    own.wait()
    all_but_one(asked, sems.at[0])
    all_but_one(wanted, sems.at[1])
    load = pltpu.make_async_copy(wanted, ids, ids_sem)
    load.start()
    load.wait()

    def gather(block):
        for j in range(slots):
            stage[pl.ds(2 * j, 2), :] = wide[ids[block, 0, j]]
        found[block] = stage[...].astype(BF16)

    gather(me)
    keep = pltpu.make_async_copy(found.at[me], fetched.at[me], own_sem)

    def serve(step, carry):
        gx, gy = peer(step)
        gather(gx * sizes[1] + gy)

        @pl.when(step > 1)
        def _():
            send(peer(step - 1), sizes, found, fetched, sems.at[2], sems.at[3])

        return carry

    lax.fori_loop(1, owners, serve, 0)
    keep.start()
    send(peer(owners - 1), sizes, found, fetched, sems.at[2], sems.at[3])
    keep.wait()
    all_but_one(found, sems.at[2])
    all_but_one(fetched, sems.at[3])


def fetch_rows(asked, table, sizes, slots):
    rows, feature = table.shape
    owners = asked.shape[0]
    hbm = pl.BlockSpec(memory_space=pltpu.HBM)
    return pl.pallas_call(
        functools.partial(fetch_kernel, sizes, slots),
        name="fetch_rows",
        out_shape=(
            jax.ShapeDtypeStruct((owners, 2 * slots, HALF), BF16),
            jax.ShapeDtypeStruct(asked.shape, jnp.int32),
        ),
        in_specs=[vmem(), hbm],
        out_specs=(hbm, vmem()),
        scratch_shapes=[
            pltpu.VMEM((rows, feature), BF16),
            pltpu.VMEM((rows + 4, 2, HALF), F32),
            pltpu.VMEM((2 * slots, HALF), F32),
            pltpu.VMEM((owners, 2 * slots, HALF), BF16),
            pltpu.SMEM(asked.shape, jnp.int32),
            pltpu.SemaphoreType.DMA,
            pltpu.SemaphoreType.DMA,
            pltpu.SemaphoreType.DMA,
            pltpu.SemaphoreType.DMA((4,)),
        ],
        compiler_params=pltpu.CompilerParams(
            collective_id=0, has_side_effects=True, vmem_limit_bytes=40 * MIB
        ),
    )(asked, table)


def exchange_kernel(sizes, given, taken, own_sem, sems):
    owners = sizes[0] * sizes[1]
    me = lax.axis_index("gx") * sizes[1] + lax.axis_index("gy")
    others = partners()
    barrier = greet(others)
    own = pltpu.make_async_copy(given.at[me], taken.at[me], own_sem)
    own.start()
    pl.semaphore_wait(barrier, owners - 1)

    for other in others:
        send(other, sizes, given, taken, sems.at[0], sems.at[1])
    own.wait()
    all_but_one(given, sems.at[0])
    all_but_one(taken, sems.at[1])


def exchange(value, sizes):
    hbm = pl.BlockSpec(memory_space=pltpu.HBM)
    return pl.pallas_call(
        functools.partial(exchange_kernel, sizes),
        name="exchange",
        out_shape=jax.ShapeDtypeStruct(value.shape, value.dtype),
        in_specs=[hbm],
        out_specs=hbm,
        scratch_shapes=[pltpu.SemaphoreType.DMA, pltpu.SemaphoreType.DMA((2,))],
        compiler_params=pltpu.CompilerParams(
            collective_id=1, has_side_effects=True, vmem_limit_bytes=40 * MIB
        ),
    )(value)


def add_lines(totals, count, batch, line_of, value_of):
    def load(n):
        lines = [line_of(n * batch + j) for j in range(batch)]
        return [(at, totals[n % 2][at, :]) for at in lines]

    held = load(0)
    for n in range(count // batch):
        later = load(n + 1) if (n + 1) * batch < count else None
        for j, (at, old) in enumerate(held):
            totals[n % 2][at, :] = old + value_of(n * batch + j)
        held = later


def return_kernel(slots, feed, ids, grads, out, total0, total1, stage):
    step = pl.program_id(0)
    chunk = grads.shape[0]
    totals = (total0, total1)
    lists = ids.shape[0] // slots
    part = lists // feed
    batch = 8

    @pl.when(step == 0)
    def _():
        def clear(c, carry):
            at = pl.ds(pl.multiple_of(c * 512, 512), 512)
            for total in totals:
                total[at, :] = jnp.zeros((512, HALF), F32)
            return carry

        lax.fori_loop(0, (total0.shape[0] - 16) // 512, clear, 0)

    @pl.when(step < feed)
    def _():
        stage[...] = grads[...].astype(F32)

        def body(c, carry):
            given = stage.at[pl.ds(pl.multiple_of(c * 2 * slots, 2 * slots), 2 * slots), :]

            add_lines(
                totals,
                slots,
                batch,
                lambda j: two(ids.at[pl.ds(j * lists, lists)][step * part + c]),
                lambda j: given[pl.ds(2 * j, 2), :],
            )
            return carry

        lax.fori_loop(0, part, body, 0)

    @pl.when(step >= feed)
    def _():
        rows = out.shape[0]
        at = pl.multiple_of((step - feed) * 2 * rows, 2 * rows)
        for h in range(2):
            lines = pl.ds(at + h, rows, stride=2)
            out[:, h * HALF : (h + 1) * HALF] = total0[lines, :] + total1[lines, :]


def return_rows(ids, grads, rows, slots):
    feed = 8
    drain = 8
    chunk = grads.shape[0] // feed
    return pl.pallas_call(
        functools.partial(return_kernel, slots, feed),
        name="return_rows",
        grid=(feed + drain,),
        out_shape=jax.ShapeDtypeStruct((rows, 2 * HALF), F32),
        in_specs=[smem(), pl.BlockSpec((chunk, HALF), lambda i: (jnp.minimum(i, feed - 1), 0))],
        out_specs=pl.BlockSpec((rows // drain, 2 * HALF), lambda i: (jnp.maximum(i - feed, 0), 0)),
        scratch_shapes=[pltpu.VMEM((2 * rows + 16, HALF), F32)] * 2 + [pltpu.VMEM((chunk, HALF), F32)],
        compiler_params=pltpu.CompilerParams(vmem_limit_bytes=40 * MIB),
    )(ids.T.reshape(-1), grads)


def route_kernel(
    interests, hist_len,
    slots, fetched, bilinear, first_logits, live, cotangent, keys,
    capsules, slot_grads,
    narrow, narrow_sems, wide, more, rows, stage_a, stage_b, logits, w0, w1, w2, z0, z1, pooled, q0, q1, g0, g1, g2, s0, s1, final,
):
    groups = live.shape[0]
    width = UG * LP
    lines = interests * UG
    feature = rows.shape[1]

    def nt(a, b):
        return lax.dot_general(a, b, (((1,), (1,)), ((), ())), preferred_element_type=F32)

    def tn(a, b):
        return lax.dot_general(a, b, (((0,), (0,)), ((), ())), preferred_element_type=F32)

    def block(g):
        return rows[pl.ds(pl.multiple_of(g * width, width), width), :]

    def lanes(ref, g):
        return ref.at[pl.ds(pl.multiple_of(g * lines, lines), lines), :]

    def users(g):
        return pl.ds(pl.multiple_of(g * UG, UG), UG)

    def by_interest(value):
        return [value[k * UG : (k + 1) * UG] for k in range(interests)]

    def gathered(ref, g):
        return jnp.concatenate([ref[k, users(g), :] for k in range(interests)], axis=0).astype(BF16)

    def put_pooled(g, value):
        for k, part in enumerate(by_interest(value)):
            pooled[k, users(g), :] = part

    def mask_of(g):
        owner = lax.broadcasted_iota(jnp.int32, (UG, width), 0)
        lane = lax.broadcasted_iota(jnp.int32, (UG, width), 1)
        alive = jnp.broadcast_to(live[pl.ds(g, 1), :], (UG, width))
        return (lane // LP == owner) & (alive > 0.0)

    def coupling(value, g):
        powers = [jnp.exp(part) for part in by_interest(value)]
        scale = 1.0 / functools.reduce(jnp.add, powers)
        mask = mask_of(g)
        return jnp.concatenate([jnp.where(mask, p * scale, 0.0) for p in powers], axis=0)

    def coupling_grad(weights, dots):
        ws, ds = by_interest(weights), by_interest(dots)
        inner = functools.reduce(jnp.add, [w * d for w, d in zip(ws, ds)])
        return jnp.concatenate([w * (d - inner) for w, d in zip(ws, ds)], axis=0)

    def loop(count, body):
        lax.fori_loop(0, count, lambda i, c: (body(i), c)[1], 0)

    def over_groups(stages, unroll=8):
        def body(i):
            ids = [i * unroll + j for j in range(unroll)]
            held = [() for _ in ids]
            for stage_fn in stages:
                held = [stage_fn(g, *h) for g, h in zip(ids, held)]

        loop(groups // unroll, body)

    def mapping(k):
        return bilinear[:, k * feature : (k + 1) * feature]

    def squash(summed):
        size = jnp.sum(summed * summed, axis=1, keepdims=True)
        root = jnp.sqrt(size + EPS)
        return size, root, root / (1.0 + size)

    def forward(keep, out):
        for k in range(interests):
            summed = jnp.dot(pooled[k].astype(BF16), mapping(k), preferred_element_type=F32)
            keep[k] = summed
            _, _, factor = squash(summed)
            out[k] = nt((summed * factor).astype(BF16), mapping(k))

    def squash_grad(summed, given):
        size, root, factor = squash(summed)
        along = jnp.sum(summed * given, axis=1, keepdims=True)
        above = 1.0 + size
        slope = 1.0 / (root * above) - 2.0 * root / (above * above)
        return given * factor + summed * (slope * along), factor

    def backward(keep, out):
        for k in range(interests):
            given = jnp.dot(pooled[k].astype(BF16), mapping(k), preferred_element_type=F32)
            grad, _ = squash_grad(keep[k], given)
            out[k] = nt(grad.astype(BF16), mapping(k))

    split_dense = 1024
    parts = narrow_sems.shape[0]
    share = fetched.shape[0] // parts

    def share_of(c):
        return pl.ds(pl.multiple_of(c * share, share), share)

    def copy_in(c):
        return pltpu.make_async_copy(fetched.at[share_of(c), :], narrow.at[share_of(c), :], narrow_sems.at[c])

    def copy_out(c):
        return pltpu.make_async_copy(narrow.at[share_of(c), :], slot_grads.at[share_of(c), :], narrow_sems.at[c])

    loop(parts, lambda c: copy_in(c).start())

    def widen(c):
        copy_in(c).wait()
        for p in range(share // split_dense):
            at = pl.ds(pl.multiple_of(c * share + p * split_dense, split_dense), split_dense)
            wide[at, :] = narrow[at, :].astype(F32)

    loop(parts, widen)
    for stage in (stage_a, stage_b):
        stage[...] = jnp.zeros_like(stage)

    def line_of(g, j):
        return two(slots.at[pl.ds(j * groups, groups)][g])

    def place(j):
        return pl.ds(2 * (j // hist_len * LP + j % hist_len), 2)

    behaviors = UG * hist_len

    def gather(g, stage):
        for j in range(behaviors):
            stage[place(j), :] = wide[line_of(g, j), :]

    def first(g, stage):
        at = pl.ds(pl.multiple_of(g * width, width), width)
        dense = jnp.concatenate(
            [stage[pl.ds(h, width, stride=2), :].astype(BF16) for h in range(2)], axis=1
        )
        rows[at, :] = dense
        start = jnp.concatenate(
            [
                jnp.broadcast_to(first_logits[pl.ds(g * interests + k, 1), :], (UG, width))
                for k in range(interests)
            ],
            axis=0,
        )
        lanes(logits, g)[...] = start
        weights = coupling(start, g)
        lanes(w0, g)[...] = weights
        put_pooled(g, jnp.dot(weights.astype(BF16), dense, preferred_element_type=F32))

    gather(0, stage_a)

    def first_pair(i):
        gather(2 * i + 1, stage_b)
        first(2 * i, stage_a)
        gather(jnp.minimum(2 * i + 2, groups - 1), stage_a)
        first(2 * i + 1, stage_b)

    loop(groups // 2, first_pair)
    forward(s0, q0)

    def turn(q, w, last):
        def agree(g):
            return (nt(gathered(q, g), block(g)),)

        def reweigh(g, scores):
            value = lanes(logits, g)[...] + scores
            if not last:
                lanes(logits, g)[...] = value
            weights = coupling(value, g)
            lanes(w, g)[...] = weights
            return (weights.astype(BF16),)

        def pool(g, weights):
            put_pooled(g, jnp.dot(weights, block(g), preferred_element_type=F32))
            return ()

        over_groups([agree, reweigh, pool])

    turn(q0, w1, False)
    forward(s1, q1)
    turn(q1, w2, True)

    for k in range(interests):
        summed = jnp.dot(pooled[k].astype(BF16), mapping(k), preferred_element_type=F32)
        grad, factor = squash_grad(summed, cotangent[k])
        final[:, k, :] = summed * factor
        g2[k] = nt(grad.astype(BF16), mapping(k))

    for u in range(0, final.shape[0], 64):
        capsules[u : u + 64] = final[u : u + 64].astype(BF16)

    def turn_back(gr, w, z, add):
        def dots(g):
            return (nt(gathered(gr, g), block(g)),)

        def reweigh(g, value):
            grad = coupling_grad(lanes(w, g)[...], value)
            if add:
                grad = grad + lanes(logits, g)[...]
            else:
                lanes(logits, g)[...] = grad
            grad = grad.astype(BF16)
            lanes(z, g)[...] = grad
            return (grad,)

        def pool(g, grad):
            put_pooled(g, jnp.dot(grad, block(g), preferred_element_type=F32))
            return ()

        over_groups([dots, reweigh, pool])

    turn_back(g2, w2, z1, False)
    backward(s1, g1)
    turn_back(g1, w1, z0, True)
    backward(s0, g0)

    def clear(c):
        at = pl.ds(pl.multiple_of(c * split_dense, split_dense), split_dense)
        for total in (wide, more):
            total[at, :] = jnp.zeros((split_dense, HALF), F32)

    loop(fetched.shape[0] // split_dense, clear)

    def spread(g, stage):
        coefs = jnp.concatenate(
            [lanes(w, g)[...].astype(BF16) for w in (w0, w1, w2)]
            + [lanes(z, g)[...] for z in (z0, z1)],
            axis=0,
        )
        basis = jnp.concatenate([gathered(b, g) for b in (g0, g1, g2, q0, q1)], axis=0)
        grads = tn(coefs, basis).astype(BF16)
        part = width // 2
        for p in range(2):
            key = keys[pl.ds(2 * g + p, 1), :]
            column = jnp.transpose(jnp.broadcast_to(key, (UG, part)))[:, :1]
            merged = jnp.dot(
                jnp.where(column == key, 1.0, 0.0).astype(BF16),
                grads[p * part : (p + 1) * part],
                preferred_element_type=F32,
            )
            for h in range(2):
                stage[pl.ds(2 * p * part + h, part, stride=2), :] = merged[:, h * HALF : (h + 1) * HALF]

    def scatter(g, stage):
        add_lines(
            (wide, more),
            behaviors,
            BATCH,
            lambda j: line_of(g, j),
            lambda j: stage[place(j), :],
        )

    spread(0, stage_a)

    def last_pair(i):
        scatter(2 * i, stage_a)
        spread(2 * i + 1, stage_b)
        scatter(2 * i + 1, stage_b)
        spread(jnp.minimum(2 * i + 2, groups - 1), stage_a)

    loop(groups // 2, last_pair)

    def emit(c):
        for p in range(share // split_dense):
            at = pl.ds(pl.multiple_of(c * share + p * split_dense, split_dense), split_dense)
            narrow[at, :] = (wide[at, :] + more[at, :]).astype(BF16)
        copy_out(c).start()

    loop(parts, emit)
    loop(parts, lambda c: copy_out(c).wait())


def route(slots, fetched, bilinear, lengths, init_logits, interest_grad):
    users_here, hist_len, interests = init_logits.shape
    feature = bilinear.shape[0]
    groups = users_here // UG
    width = UG * LP
    pad = LP - hist_len
    batch = jnp.arange(hist_len, dtype=jnp.int32) // BATCH + LP * (jnp.arange(users_here) % 4)[:, None]
    keys = (slots * (4 * LP) + batch).astype(F32)
    keys = jnp.pad(keys, ((0, 0), (0, pad)), constant_values=-1.0).reshape(-1, 4 * LP)
    live = (jnp.arange(LP, dtype=jnp.int32)[None, :] < lengths[:, None]).astype(F32)
    live = live.reshape(groups, width)
    first_logits = jnp.pad(jnp.transpose(init_logits, (0, 2, 1)), ((0, 0), (0, 0), (0, pad)))
    first_logits = first_logits.reshape(groups, UG, interests, LP)
    first_logits = jnp.transpose(first_logits, (0, 2, 1, 3)).reshape(groups * interests, width)
    cotangent = jnp.transpose(interest_grad, (1, 0, 2))
    lines = groups * interests * UG
    lines_of = (2 * slots).reshape(groups, UG * hist_len).T.reshape(-1)
    per_user = pltpu.VMEM((interests, users_here, feature), F32)
    hbm = pl.BlockSpec(memory_space=pltpu.HBM)
    capsules, slot_grads = pl.pallas_call(
        functools.partial(route_kernel, interests, hist_len),
        name="route_users",
        out_shape=(
            jax.ShapeDtypeStruct((users_here, interests, feature), BF16),
            jax.ShapeDtypeStruct(fetched.shape, BF16),
        ),
        in_specs=[smem(), hbm] + [vmem()] * 5,
        out_specs=(vmem(), hbm),
        scratch_shapes=[
            pltpu.VMEM(fetched.shape, BF16),
            pltpu.SemaphoreType.DMA((8,)),
            pltpu.VMEM(fetched.shape, F32),
            pltpu.VMEM(fetched.shape, F32),
            pltpu.VMEM((users_here * LP, feature), BF16),
            pltpu.VMEM((2 * width, HALF), F32),
            pltpu.VMEM((2 * width, HALF), F32),
        ]
        + [pltpu.VMEM((lines, width), F32)] * 4
        + [pltpu.VMEM((lines, width), BF16)] * 2
        + [per_user] * 8
        + [pltpu.VMEM((users_here, interests, feature), F32)],
        compiler_params=pltpu.CompilerParams(vmem_limit_bytes=60 * MIB),
    )(lines_of, fetched, bilinear, first_logits, live, cotangent, keys)
    return capsules, slot_grads


def local(sizes, item_table, bilinear, requests, history, lengths, init_logits, interest_grad):
    asked = requests[0]
    owners, slots = asked.shape
    table_rows = item_table.shape[0]
    asked = jnp.where(asked >= 0, asked, table_rows)
    asked = jnp.pad(asked, ((0, 0), (0, 128 - slots)))[:, None, :]
    fetched, wanted = fetch_rows(asked, item_table, sizes, slots)
    fetched = fetched.reshape(-1, HALF)
    capsules, slot_grads = route(history, fetched, bilinear, lengths, init_logits, interest_grad)
    returned = exchange(slot_grads.reshape(owners, 2 * slots, HALF), sizes).reshape(-1, HALF)
    return capsules, return_rows(2 * wanted[:, 0, :slots], returned, table_rows, slots)


def solution(mesh):
    both = ("gx", "gy")
    placed = (
        P(both, None),
        P(),
        P(both, None, None),
        P(both, None),
        P(both),
        P(both, None, None),
        P(both, None, None),
    )
    return jax.shard_map(
        functools.partial(local, (mesh.shape["gx"], mesh.shape["gy"])),
        mesh=mesh,
        in_specs=placed,
        out_specs=(P(both, None, None), P(both, None)),
        check_vma=False,
    )
```

```python
import functools

import jax
import jax.numpy as jnp
from jax import lax
from jax.experimental import pallas as pl
from jax.experimental.pallas import tpu as pltpu
from jax.sharding import PartitionSpec as P

ITERS = 3
EPS = 1e-06
LP = 64
UG = 8
BATCH = 5
HALF = 128
MIB = 1024 * 1024
F32 = jnp.float32
BF16 = jnp.bfloat16
MESH = pl.DeviceIdType.MESH


def vmem():
    return pl.BlockSpec(memory_space=pltpu.VMEM)


def smem():
    return pl.BlockSpec(memory_space=pltpu.SMEM)


def two(i):
    return pl.ds(pl.multiple_of(i, 2), 2)


def peer(step):
    a, b, c, d = step % 4, step // 4 % 4, step // 16 % 4, step // 64
    gx, gy = lax.axis_index("gx"), lax.axis_index("gy")
    z = (gx // 2 + a + b) % 4
    core = (gx + a // 2 + d) % 2
    y = (gy // 4 + a + b + c) % 4
    x = (gy + a) % 4
    return z * 2 + core, y * 4 + x


def partners():
    gx, gy = lax.axis_index("gx"), lax.axis_index("gy")
    z = [(gx // 2 + i) % 4 * 2 for i in range(4)]
    core = [(gx + i) % 2 for i in range(2)]
    y = [(gy // 4 + i) % 4 * 4 for i in range(4)]
    x = [(gy + i) % 4 for i in range(4)]
    found = []
    for step in range(1, 128):
        a, b, c, d = step % 4, step // 4 % 4, step // 16 % 4, step // 64
        found.append((z[(a + b) % 4] + core[(a // 2 + d) % 2], y[(a + b + c) % 4] + x[a]))
    return found


def greet(others):
    barrier = pltpu.get_barrier_semaphore()
    for other in others:
        pl.semaphore_signal(barrier, inc=1, device_id=other, device_id_type=MESH)
    return barrier


def send(other, sizes, source, target, send_sem, recv_sem):
    gx, gy = other
    me = lax.axis_index("gx") * sizes[1] + lax.axis_index("gy")
    pltpu.make_async_remote_copy(
        src_ref=source.at[gx * sizes[1] + gy],
        dst_ref=target.at[me],
        send_sem=send_sem,
        recv_sem=recv_sem,
        device_id=(gx, gy),
        device_id_type=MESH,
    ).start()


def all_but_one(ref, sem):
    part = ref.at[pl.ds(0, ref.shape[0] - 1)]
    pltpu.make_async_copy(part, part, sem).wait()


def fetch_kernel(
    sizes, slots, asked, table, fetched, wanted,
    narrow, wide, stage, found, ids, table_sem, own_sem, ids_sem, sems,
):
    owners = sizes[0] * sizes[1]
    rows = table.shape[0]
    me = lax.axis_index("gx") * sizes[1] + lax.axis_index("gy")
    fill = pltpu.make_async_copy(table, narrow, table_sem)
    fill.start()
    own = pltpu.make_async_copy(asked.at[me], wanted.at[me], own_sem)
    own.start()
    others = partners()
    barrier = greet(others)
    fill.wait()

    def widen(c, carry):
        at = pl.ds(pl.multiple_of(c * 512, 512), 512)
        for h in range(2):
            wide[at, h, :] = narrow[at, h * HALF : (h + 1) * HALF].astype(F32)
        return carry

    early = rows // 512 * 5 // 8
    lax.fori_loop(0, early, widen, 0)
    pl.semaphore_wait(barrier, owners - 1)

    for other in others:
        send(other, sizes, asked, wanted, sems.at[0], sems.at[1])
    lax.fori_loop(early, rows // 512, widen, 0)
    wide[rows] = jnp.zeros((2, HALF), F32)
    own.wait()
    all_but_one(asked, sems.at[0])
    all_but_one(wanted, sems.at[1])
    load = pltpu.make_async_copy(wanted, ids, ids_sem)
    load.start()
    load.wait()

    def gather(block):
        for j in range(slots):
            stage[pl.ds(2 * j, 2), :] = wide[ids[block, 0, j]]
        found[block] = stage[...].astype(BF16)

    gather(me)
    keep = pltpu.make_async_copy(found.at[me], fetched.at[me], own_sem)

    def serve(step, carry):
        gx, gy = peer(step)
        gather(gx * sizes[1] + gy)

        @pl.when(step > 1)
        def _():
            send(peer(step - 1), sizes, found, fetched, sems.at[2], sems.at[3])

        return carry

    lax.fori_loop(1, owners, serve, 0)
    keep.start()
    send(peer(owners - 1), sizes, found, fetched, sems.at[2], sems.at[3])
    keep.wait()
    all_but_one(found, sems.at[2])
    all_but_one(fetched, sems.at[3])


def fetch_rows(asked, table, sizes, slots):
    rows, feature = table.shape
    owners = asked.shape[0]
    hbm = pl.BlockSpec(memory_space=pltpu.HBM)
    return pl.pallas_call(
        functools.partial(fetch_kernel, sizes, slots),
        name="fetch_rows",
        out_shape=(
            jax.ShapeDtypeStruct((owners, 2 * slots, HALF), BF16),
            jax.ShapeDtypeStruct(asked.shape, jnp.int32),
        ),
        in_specs=[vmem(), hbm],
        out_specs=(hbm, vmem()),
        scratch_shapes=[
            pltpu.VMEM((rows, feature), BF16),
            pltpu.VMEM((rows + 4, 2, HALF), F32),
            pltpu.VMEM((2 * slots, HALF), F32),
            pltpu.VMEM((owners, 2 * slots, HALF), BF16),
            pltpu.SMEM(asked.shape, jnp.int32),
            pltpu.SemaphoreType.DMA,
            pltpu.SemaphoreType.DMA,
            pltpu.SemaphoreType.DMA,
            pltpu.SemaphoreType.DMA((4,)),
        ],
        compiler_params=pltpu.CompilerParams(
            collective_id=0, has_side_effects=True, vmem_limit_bytes=61 * MIB
        ),
    )(asked, table)


def exchange_kernel(sizes, given, taken, own_sem, sems):
    owners = sizes[0] * sizes[1]
    me = lax.axis_index("gx") * sizes[1] + lax.axis_index("gy")
    others = partners()
    barrier = greet(others)
    own = pltpu.make_async_copy(given.at[me], taken.at[me], own_sem)
    own.start()
    pl.semaphore_wait(barrier, owners - 1)

    for other in others:
        send(other, sizes, given, taken, sems.at[0], sems.at[1])
    own.wait()
    all_but_one(given, sems.at[0])
    all_but_one(taken, sems.at[1])


def exchange(value, sizes):
    hbm = pl.BlockSpec(memory_space=pltpu.HBM)
    return pl.pallas_call(
        functools.partial(exchange_kernel, sizes),
        name="exchange",
        out_shape=jax.ShapeDtypeStruct(value.shape, value.dtype),
        in_specs=[hbm],
        out_specs=hbm,
        scratch_shapes=[pltpu.SemaphoreType.DMA, pltpu.SemaphoreType.DMA((2,))],
        compiler_params=pltpu.CompilerParams(
            collective_id=1, has_side_effects=True, vmem_limit_bytes=61 * MIB
        ),
    )(value)


def add_lines(totals, count, batch, line_of, value_of):
    def load(n):
        lines = [line_of(n * batch + j) for j in range(batch)]
        return [(at, totals[n % 2][at, :]) for at in lines]

    held = load(0)
    for n in range(count // batch):
        later = load(n + 1) if (n + 1) * batch < count else None
        for j, (at, old) in enumerate(held):
            totals[n % 2][at, :] = old + value_of(n * batch + j)
        held = later


def return_kernel(slots, feed, ids, grads, out, total0, total1, stage):
    step = pl.program_id(0)
    chunk = grads.shape[0]
    totals = (total0, total1)
    lists = ids.shape[0] // slots
    part = lists // feed
    batch = 8

    @pl.when(step == 0)
    def _():
        def clear(c, carry):
            at = pl.ds(pl.multiple_of(c * 512, 512), 512)
            for total in totals:
                total[at, :] = jnp.zeros((512, HALF), F32)
            return carry

        lax.fori_loop(0, (total0.shape[0] - 16) // 512, clear, 0)

    @pl.when(step < feed)
    def _():
        stage[...] = grads[...].astype(F32)

        def body(c, carry):
            given = stage.at[pl.ds(pl.multiple_of(c * 2 * slots, 2 * slots), 2 * slots), :]

            add_lines(
                totals,
                slots,
                batch,
                lambda j: two(ids.at[pl.ds(j * lists, lists)][step * part + c]),
                lambda j: given[pl.ds(2 * j, 2), :],
            )
            return carry

        lax.fori_loop(0, part, body, 0)

    @pl.when(step >= feed)
    def _():
        rows = out.shape[0]
        at = pl.multiple_of((step - feed) * 2 * rows, 2 * rows)
        for h in range(2):
            lines = pl.ds(at + h, rows, stride=2)
            out[:, h * HALF : (h + 1) * HALF] = total0[lines, :] + total1[lines, :]


def return_rows(ids, grads, rows, slots):
    feed = 8
    drain = 8
    chunk = grads.shape[0] // feed
    return pl.pallas_call(
        functools.partial(return_kernel, slots, feed),
        name="return_rows",
        grid=(feed + drain,),
        out_shape=jax.ShapeDtypeStruct((rows, 2 * HALF), F32),
        in_specs=[smem(), pl.BlockSpec((chunk, HALF), lambda i: (jnp.minimum(i, feed - 1), 0))],
        out_specs=pl.BlockSpec((rows // drain, 2 * HALF), lambda i: (jnp.maximum(i - feed, 0), 0)),
        scratch_shapes=[pltpu.VMEM((2 * rows + 16, HALF), F32)] * 2 + [pltpu.VMEM((chunk, HALF), F32)],
        compiler_params=pltpu.CompilerParams(vmem_limit_bytes=61 * MIB),
    )(ids.T.reshape(-1), grads)


def route_kernel(
    interests, hist_len,
    slots, fetched, bilinear, first_logits, live, cotangent, keys,
    capsules, slot_grads,
    narrow, narrow_sems, wide, more, rows, stage_a, stage_b, logits, w0, w1, w2, z0, z1, pooled, q0, q1, g0, g1, g2, s0, s1, final,
):
    groups = live.shape[0]
    width = UG * LP
    lines = interests * UG
    feature = rows.shape[1]

    def nt(a, b):
        return lax.dot_general(a, b, (((1,), (1,)), ((), ())), preferred_element_type=F32)

    def tn(a, b):
        return lax.dot_general(a, b, (((0,), (0,)), ((), ())), preferred_element_type=F32)

    def block(g):
        return rows[pl.ds(pl.multiple_of(g * width, width), width), :]

    def lanes(ref, g):
        return ref.at[pl.ds(pl.multiple_of(g * lines, lines), lines), :]

    def users(g):
        return pl.ds(pl.multiple_of(g * UG, UG), UG)

    def by_interest(value):
        return [value[k * UG : (k + 1) * UG] for k in range(interests)]

    def gathered(ref, g):
        return jnp.concatenate([ref[k, users(g), :] for k in range(interests)], axis=0).astype(BF16)

    def put_pooled(g, value):
        for k, part in enumerate(by_interest(value)):
            pooled[k, users(g), :] = part

    def mask_of(g):
        owner = lax.broadcasted_iota(jnp.int32, (UG, width), 0)
        lane = lax.broadcasted_iota(jnp.int32, (UG, width), 1)
        alive = jnp.broadcast_to(live[pl.ds(g, 1), :], (UG, width))
        return (lane // LP == owner) & (alive > 0.0)

    def coupling(value, g):
        powers = [jnp.exp(part) for part in by_interest(value)]
        scale = 1.0 / functools.reduce(jnp.add, powers)
        mask = mask_of(g)
        return jnp.concatenate([jnp.where(mask, p * scale, 0.0) for p in powers], axis=0)

    def coupling_grad(weights, dots):
        ws, ds = by_interest(weights), by_interest(dots)
        inner = functools.reduce(jnp.add, [w * d for w, d in zip(ws, ds)])
        return jnp.concatenate([w * (d - inner) for w, d in zip(ws, ds)], axis=0)

    def loop(count, body):
        lax.fori_loop(0, count, lambda i, c: (body(i), c)[1], 0)

    def over_groups(stages, unroll=8):
        def body(i):
            ids = [i * unroll + j for j in range(unroll)]
            held = [() for _ in ids]
            for stage_fn in stages:
                held = [stage_fn(g, *h) for g, h in zip(ids, held)]

        loop(groups // unroll, body)

    def mapping(k):
        return bilinear[:, k * feature : (k + 1) * feature]

    def squash(summed):
        size = jnp.sum(summed * summed, axis=1, keepdims=True)
        root = jnp.sqrt(size + EPS)
        return size, root, root / (1.0 + size)

    def forward(keep, out):
        for k in range(interests):
            summed = jnp.dot(pooled[k].astype(BF16), mapping(k), preferred_element_type=F32)
            keep[k] = summed
            _, _, factor = squash(summed)
            out[k] = nt((summed * factor).astype(BF16), mapping(k))

    def squash_grad(summed, given):
        size, root, factor = squash(summed)
        along = jnp.sum(summed * given, axis=1, keepdims=True)
        above = 1.0 + size
        slope = 1.0 / (root * above) - 2.0 * root / (above * above)
        return given * factor + summed * (slope * along), factor

    def backward(keep, out):
        for k in range(interests):
            given = jnp.dot(pooled[k].astype(BF16), mapping(k), preferred_element_type=F32)
            grad, _ = squash_grad(keep[k], given)
            out[k] = nt(grad.astype(BF16), mapping(k))

    split_dense = 1024
    parts = narrow_sems.shape[0]
    share = fetched.shape[0] // parts

    def share_of(c):
        return pl.ds(pl.multiple_of(c * share, share), share)

    def copy_in(c):
        return pltpu.make_async_copy(fetched.at[share_of(c), :], narrow.at[share_of(c), :], narrow_sems.at[c])

    def copy_out(c):
        return pltpu.make_async_copy(narrow.at[share_of(c), :], slot_grads.at[share_of(c), :], narrow_sems.at[c])

    loop(parts, lambda c: copy_in(c).start())

    def widen(c):
        copy_in(c).wait()
        for p in range(share // split_dense):
            at = pl.ds(pl.multiple_of(c * share + p * split_dense, split_dense), split_dense)
            wide[at, :] = narrow[at, :].astype(F32)

    loop(parts, widen)
    for stage in (stage_a, stage_b):
        stage[...] = jnp.zeros_like(stage)

    def line_of(g, j):
        return two(slots.at[pl.ds(j * groups, groups)][g])

    def place(j):
        return pl.ds(2 * (j // hist_len * LP + j % hist_len), 2)

    behaviors = UG * hist_len

    def gather(g, stage):
        for j in range(behaviors):
            stage[place(j), :] = wide[line_of(g, j), :]

    def first(g, stage):
        at = pl.ds(pl.multiple_of(g * width, width), width)
        dense = jnp.concatenate(
            [stage[pl.ds(h, width, stride=2), :].astype(BF16) for h in range(2)], axis=1
        )
        rows[at, :] = dense
        start = jnp.concatenate(
            [
                jnp.broadcast_to(first_logits[pl.ds(g * interests + k, 1), :], (UG, width))
                for k in range(interests)
            ],
            axis=0,
        )
        lanes(logits, g)[...] = start
        weights = coupling(start, g)
        lanes(w0, g)[...] = weights
        put_pooled(g, jnp.dot(weights.astype(BF16), dense, preferred_element_type=F32))

    gather(0, stage_a)

    def first_pair(i):
        gather(2 * i + 1, stage_b)
        first(2 * i, stage_a)
        gather(jnp.minimum(2 * i + 2, groups - 1), stage_a)
        first(2 * i + 1, stage_b)

    loop(groups // 2, first_pair)
    forward(s0, q0)

    def turn(q, w, last):
        def agree(g):
            return (nt(gathered(q, g), block(g)),)

        def reweigh(g, scores):
            value = lanes(logits, g)[...] + scores
            if not last:
                lanes(logits, g)[...] = value
            weights = coupling(value, g)
            lanes(w, g)[...] = weights
            return (weights.astype(BF16),)

        def pool(g, weights):
            put_pooled(g, jnp.dot(weights, block(g), preferred_element_type=F32))
            return ()

        over_groups([agree, reweigh, pool])

    turn(q0, w1, False)
    forward(s1, q1)
    turn(q1, w2, True)

    for k in range(interests):
        summed = jnp.dot(pooled[k].astype(BF16), mapping(k), preferred_element_type=F32)
        grad, factor = squash_grad(summed, cotangent[k])
        final[:, k, :] = summed * factor
        g2[k] = nt(grad.astype(BF16), mapping(k))

    for u in range(0, final.shape[0], 64):
        capsules[u : u + 64] = final[u : u + 64].astype(BF16)

    def turn_back(gr, w, z, add):
        def dots(g):
            return (nt(gathered(gr, g), block(g)),)

        def reweigh(g, value):
            grad = coupling_grad(lanes(w, g)[...], value)
            if add:
                grad = grad + lanes(logits, g)[...]
            else:
                lanes(logits, g)[...] = grad
            grad = grad.astype(BF16)
            lanes(z, g)[...] = grad
            return (grad,)

        def pool(g, grad):
            put_pooled(g, jnp.dot(grad, block(g), preferred_element_type=F32))
            return ()

        over_groups([dots, reweigh, pool])

    turn_back(g2, w2, z1, False)
    backward(s1, g1)
    turn_back(g1, w1, z0, True)
    backward(s0, g0)

    def clear(c):
        at = pl.ds(pl.multiple_of(c * split_dense, split_dense), split_dense)
        for total in (wide, more):
            total[at, :] = jnp.zeros((split_dense, HALF), F32)

    loop(fetched.shape[0] // split_dense, clear)

    def spread(g, stage):
        coefs = jnp.concatenate(
            [lanes(w, g)[...].astype(BF16) for w in (w0, w1, w2)]
            + [lanes(z, g)[...] for z in (z0, z1)],
            axis=0,
        )
        basis = jnp.concatenate([gathered(b, g) for b in (g0, g1, g2, q0, q1)], axis=0)
        grads = tn(coefs, basis).astype(BF16)
        part = width // 2
        for p in range(2):
            key = keys[pl.ds(2 * g + p, 1), :]
            column = jnp.transpose(jnp.broadcast_to(key, (UG, part)))[:, :1]
            merged = jnp.dot(
                jnp.where(column == key, 1.0, 0.0).astype(BF16),
                grads[p * part : (p + 1) * part],
                preferred_element_type=F32,
            )
            for h in range(2):
                stage[pl.ds(2 * p * part + h, part, stride=2), :] = merged[:, h * HALF : (h + 1) * HALF]

    def scatter(g, stage):
        add_lines(
            (wide, more),
            behaviors,
            BATCH,
            lambda j: line_of(g, j),
            lambda j: stage[place(j), :],
        )

    spread(0, stage_a)

    def last_pair(i):
        scatter(2 * i, stage_a)
        spread(2 * i + 1, stage_b)
        scatter(2 * i + 1, stage_b)
        spread(jnp.minimum(2 * i + 2, groups - 1), stage_a)

    loop(groups // 2, last_pair)

    def emit(c):
        for p in range(share // split_dense):
            at = pl.ds(pl.multiple_of(c * share + p * split_dense, split_dense), split_dense)
            narrow[at, :] = (wide[at, :] + more[at, :]).astype(BF16)
        copy_out(c).start()

    loop(parts, emit)
    loop(parts, lambda c: copy_out(c).wait())


def route(slots, fetched, bilinear, lengths, init_logits, interest_grad):
    users_here, hist_len, interests = init_logits.shape
    feature = bilinear.shape[0]
    groups = users_here // UG
    width = UG * LP
    pad = LP - hist_len
    batch = jnp.arange(hist_len, dtype=jnp.int32) + hist_len * (jnp.arange(users_here) % 4)[:, None]
    batch = batch // BATCH
    keys = (slots * (4 * LP) + batch).astype(F32)
    keys = jnp.pad(keys, ((0, 0), (0, pad)), constant_values=-1.0).reshape(-1, 4 * LP)
    live = (jnp.arange(LP, dtype=jnp.int32)[None, :] < lengths[:, None]).astype(F32)
    live = live.reshape(groups, width)
    first_logits = jnp.pad(jnp.transpose(init_logits, (0, 2, 1)), ((0, 0), (0, 0), (0, pad)))
    first_logits = first_logits.reshape(groups, UG, interests, LP)
    first_logits = jnp.transpose(first_logits, (0, 2, 1, 3)).reshape(groups * interests, width)
    cotangent = jnp.transpose(interest_grad, (1, 0, 2))
    lines = groups * interests * UG
    lines_of = (2 * slots).reshape(groups, UG * hist_len).T.reshape(-1)
    per_user = pltpu.VMEM((interests, users_here, feature), F32)
    hbm = pl.BlockSpec(memory_space=pltpu.HBM)
    capsules, slot_grads = pl.pallas_call(
        functools.partial(route_kernel, interests, hist_len),
        name="route_users",
        out_shape=(
            jax.ShapeDtypeStruct((users_here, interests, feature), BF16),
            jax.ShapeDtypeStruct(fetched.shape, BF16),
        ),
        in_specs=[smem(), hbm] + [vmem()] * 5,
        out_specs=(vmem(), hbm),
        scratch_shapes=[
            pltpu.VMEM(fetched.shape, BF16),
            pltpu.SemaphoreType.DMA((8,)),
            pltpu.VMEM(fetched.shape, F32),
            pltpu.VMEM(fetched.shape, F32),
            pltpu.VMEM((users_here * LP, feature), BF16),
            pltpu.VMEM((2 * width, HALF), F32),
            pltpu.VMEM((2 * width, HALF), F32),
        ]
        + [pltpu.VMEM((lines, width), F32)] * 4
        + [pltpu.VMEM((lines, width), BF16)] * 2
        + [per_user] * 8
        + [pltpu.VMEM((users_here, interests, feature), F32)],
        compiler_params=pltpu.CompilerParams(vmem_limit_bytes=61 * MIB),
    )(lines_of, fetched, bilinear, first_logits, live, cotangent, keys)
    return capsules, slot_grads


def local(sizes, item_table, bilinear, requests, history, lengths, init_logits, interest_grad):
    asked = requests[0]
    owners, slots = asked.shape
    table_rows = item_table.shape[0]
    asked = jnp.where(asked >= 0, asked, table_rows)
    asked = jnp.pad(asked, ((0, 0), (0, 128 - slots)))[:, None, :]
    fetched, wanted = fetch_rows(asked, item_table, sizes, slots)
    fetched = fetched.reshape(-1, HALF)
    capsules, slot_grads = route(history, fetched, bilinear, lengths, init_logits, interest_grad)
    returned = exchange(slot_grads.reshape(owners, 2 * slots, HALF), sizes).reshape(-1, HALF)
    return capsules, return_rows(2 * wanted[:, 0, :slots], returned, table_rows, slots)


def solution(mesh):
    both = ("gx", "gy")
    placed = (
        P(both, None),
        P(),
        P(both, None, None),
        P(both, None),
        P(both),
        P(both, None, None),
        P(both, None, None),
    )
    return jax.shard_map(
        functools.partial(local, (mesh.shape["gx"], mesh.shape["gy"])),
        mesh=mesh,
        in_specs=placed,
        out_specs=(P(both, None, None), P(both, None)),
        check_vma=False,
    )
```

```python
import functools

import jax
import jax.numpy as jnp
from jax import lax
from jax.experimental import pallas as pl
from jax.experimental.pallas import tpu as pltpu
from jax.sharding import PartitionSpec as P

ITERS = 3
EPS = 1e-06
LP = 64
UG = 8
BATCH = 5
HALF = 128
MIB = 1024 * 1024
F32 = jnp.float32
BF16 = jnp.bfloat16
MESH = pl.DeviceIdType.MESH


def vmem():
    return pl.BlockSpec(memory_space=pltpu.VMEM)


def smem():
    return pl.BlockSpec(memory_space=pltpu.SMEM)


def two(i):
    return pl.ds(pl.multiple_of(i, 2), 2)


def peer(step):
    a, b, c, d = step % 4, step // 4 % 4, step // 16 % 4, step // 64
    gx, gy = lax.axis_index("gx"), lax.axis_index("gy")
    z = (gx // 2 + a + b) % 4
    core = (gx + a // 2 + d) % 2
    y = (gy // 4 + a + b + c) % 4
    x = (gy + a) % 4
    return z * 2 + core, y * 4 + x


def partners():
    gx, gy = lax.axis_index("gx"), lax.axis_index("gy")
    z = [(gx // 2 + i) % 4 * 2 for i in range(4)]
    core = [(gx + i) % 2 for i in range(2)]
    y = [(gy // 4 + i) % 4 * 4 for i in range(4)]
    x = [(gy + i) % 4 for i in range(4)]
    found = []
    for step in range(1, 128):
        a, b, c, d = step % 4, step // 4 % 4, step // 16 % 4, step // 64
        found.append((z[(a + b) % 4] + core[(a // 2 + d) % 2], y[(a + b + c) % 4] + x[a]))
    return found


def greet(others):
    barrier = pltpu.get_barrier_semaphore()
    for other in others:
        pl.semaphore_signal(barrier, inc=1, device_id=other, device_id_type=MESH)
    return barrier


def send(other, sizes, source, target, send_sem, recv_sem):
    gx, gy = other
    me = lax.axis_index("gx") * sizes[1] + lax.axis_index("gy")
    pltpu.make_async_remote_copy(
        src_ref=source.at[gx * sizes[1] + gy],
        dst_ref=target.at[me],
        send_sem=send_sem,
        recv_sem=recv_sem,
        device_id=(gx, gy),
        device_id_type=MESH,
    ).start()


def all_but_one(ref, sem):
    part = ref.at[pl.ds(0, ref.shape[0] - 1)]
    pltpu.make_async_copy(part, part, sem).wait()


def fetch_kernel(
    sizes, slots, asked, table, fetched, wanted,
    narrow, wide, stage, found, ids, table_sem, own_sem, ids_sem, sems,
):
    owners = sizes[0] * sizes[1]
    rows = table.shape[0]
    me = lax.axis_index("gx") * sizes[1] + lax.axis_index("gy")
    fill = pltpu.make_async_copy(table, narrow, table_sem)
    fill.start()
    own = pltpu.make_async_copy(asked.at[me], wanted.at[me], own_sem)
    own.start()
    others = partners()
    barrier = greet(others)
    fill.wait()

    def widen(c, carry):
        at = pl.ds(pl.multiple_of(c * 512, 512), 512)
        for h in range(2):
            wide[at, h, :] = narrow[at, h * HALF : (h + 1) * HALF].astype(F32)
        return carry

    early = rows // 512 * 5 // 8
    lax.fori_loop(0, early, widen, 0)
    pl.semaphore_wait(barrier, owners - 1)

    for other in others:
        send(other, sizes, asked, wanted, sems.at[0], sems.at[1])
    lax.fori_loop(early, rows // 512, widen, 0)
    own.wait()
    all_but_one(asked, sems.at[0])
    all_but_one(wanted, sems.at[1])
    load = pltpu.make_async_copy(wanted, ids, ids_sem)
    load.start()
    load.wait()

    def gather(block):
        for j in range(slots):
            stage[pl.ds(2 * j, 2), :] = wide[jnp.maximum(ids[block, 0, j], 0)]
        found[block] = stage[...].astype(BF16)

    gather(me)
    keep = pltpu.make_async_copy(found.at[me], fetched.at[me], own_sem)

    def serve(step, carry):
        gx, gy = peer(step)
        gather(gx * sizes[1] + gy)

        @pl.when(step > 1)
        def _():
            send(peer(step - 1), sizes, found, fetched, sems.at[2], sems.at[3])

        return carry

    lax.fori_loop(1, owners, serve, 0)
    keep.start()
    send(peer(owners - 1), sizes, found, fetched, sems.at[2], sems.at[3])
    keep.wait()
    all_but_one(found, sems.at[2])
    all_but_one(fetched, sems.at[3])


def fetch_rows(asked, table, sizes, slots):
    rows, feature = table.shape
    owners = asked.shape[0]
    hbm = pl.BlockSpec(memory_space=pltpu.HBM)
    return pl.pallas_call(
        functools.partial(fetch_kernel, sizes, slots),
        name="fetch_rows",
        out_shape=(
            jax.ShapeDtypeStruct((owners, 2 * slots, HALF), BF16),
            jax.ShapeDtypeStruct(asked.shape, jnp.int32),
        ),
        in_specs=[vmem(), hbm],
        out_specs=(hbm, vmem()),
        scratch_shapes=[
            pltpu.VMEM((rows, feature), BF16),
            pltpu.VMEM((rows, 2, HALF), F32),
            pltpu.VMEM((2 * slots, HALF), F32),
            pltpu.VMEM((owners, 2 * slots, HALF), BF16),
            pltpu.SMEM(asked.shape, jnp.int32),
            pltpu.SemaphoreType.DMA,
            pltpu.SemaphoreType.DMA,
            pltpu.SemaphoreType.DMA,
            pltpu.SemaphoreType.DMA((4,)),
        ],
        compiler_params=pltpu.CompilerParams(
            collective_id=0, has_side_effects=True, vmem_limit_bytes=61 * MIB
        ),
    )(asked, table)


def exchange_kernel(sizes, given, taken, own_sem, sems):
    owners = sizes[0] * sizes[1]
    me = lax.axis_index("gx") * sizes[1] + lax.axis_index("gy")
    others = partners()
    barrier = greet(others)
    own = pltpu.make_async_copy(given.at[me], taken.at[me], own_sem)
    own.start()
    pl.semaphore_wait(barrier, owners - 1)

    for other in others:
        send(other, sizes, given, taken, sems.at[0], sems.at[1])
    own.wait()
    all_but_one(given, sems.at[0])
    all_but_one(taken, sems.at[1])


def exchange(value, sizes):
    hbm = pl.BlockSpec(memory_space=pltpu.HBM)
    return pl.pallas_call(
        functools.partial(exchange_kernel, sizes),
        name="exchange",
        out_shape=jax.ShapeDtypeStruct(value.shape, value.dtype),
        in_specs=[hbm],
        out_specs=hbm,
        scratch_shapes=[pltpu.SemaphoreType.DMA, pltpu.SemaphoreType.DMA((2,))],
        compiler_params=pltpu.CompilerParams(
            collective_id=1, has_side_effects=True, vmem_limit_bytes=61 * MIB
        ),
    )(value)


def add_lines(totals, count, batch, line_of, value_of):
    def load(n):
        lines = [line_of(n * batch + j) for j in range(batch)]
        return [(at, totals[n % 2][at, :]) for at in lines]

    held = load(0)
    for n in range(count // batch):
        later = load(n + 1) if (n + 1) * batch < count else None
        for j, (at, old) in enumerate(held):
            totals[n % 2][at, :] = old + value_of(n * batch + j)
        held = later


def return_kernel(slots, feed, ids, grads, out, total0, total1, stage):
    step = pl.program_id(0)
    chunk = grads.shape[0]
    totals = (total0, total1)
    lists = ids.shape[0] // slots
    part = lists // feed
    batch = 8

    @pl.when(step == 0)
    def _():
        def clear(c, carry):
            at = pl.ds(pl.multiple_of(c * 512, 512), 512)
            for total in totals:
                total[at, :] = jnp.zeros((512, HALF), F32)
            return carry

        lax.fori_loop(0, (total0.shape[0] - 16) // 512, clear, 0)

    @pl.when(step < feed)
    def _():
        stage[...] = grads[...].astype(F32)

        def body(c, carry):
            given = stage.at[pl.ds(pl.multiple_of(c * 2 * slots, 2 * slots), 2 * slots), :]

            add_lines(
                totals,
                slots,
                batch,
                lambda j: two(ids.at[pl.ds(j * lists, lists)][step * part + c]),
                lambda j: given[pl.ds(2 * j, 2), :],
            )
            return carry

        lax.fori_loop(0, part, body, 0)

    @pl.when(step >= feed)
    def _():
        rows = out.shape[0]
        at = pl.multiple_of((step - feed) * 2 * rows, 2 * rows)
        for h in range(2):
            lines = pl.ds(at + h, rows, stride=2)
            out[:, h * HALF : (h + 1) * HALF] = total0[lines, :] + total1[lines, :]


def return_rows(ids, grads, rows, slots):
    feed = 8
    drain = 8
    chunk = grads.shape[0] // feed
    return pl.pallas_call(
        functools.partial(return_kernel, slots, feed),
        name="return_rows",
        grid=(feed + drain,),
        out_shape=jax.ShapeDtypeStruct((rows, 2 * HALF), F32),
        in_specs=[smem(), pl.BlockSpec((chunk, HALF), lambda i: (jnp.minimum(i, feed - 1), 0))],
        out_specs=pl.BlockSpec((rows // drain, 2 * HALF), lambda i: (jnp.maximum(i - feed, 0), 0)),
        scratch_shapes=[pltpu.VMEM((2 * rows + 16, HALF), F32)] * 2 + [pltpu.VMEM((chunk, HALF), F32)],
        compiler_params=pltpu.CompilerParams(vmem_limit_bytes=61 * MIB),
    )(ids.T.reshape(-1), grads)


def route_kernel(
    interests, hist_len,
    slots, fetched, bilinear, first_logits, live, cotangent, keys,
    capsules, slot_grads,
    narrow, narrow_sems, wide, more, rows, stage_a, stage_b, logits, w0, w1, w2, z0, z1, pooled, q0, q1, g0, g1, g2, s0, s1, final,
):
    groups = live.shape[0]
    width = UG * LP
    lines = interests * UG
    feature = rows.shape[1]

    def nt(a, b):
        return lax.dot_general(a, b, (((1,), (1,)), ((), ())), preferred_element_type=F32)

    def tn(a, b):
        return lax.dot_general(a, b, (((0,), (0,)), ((), ())), preferred_element_type=F32)

    def block(g):
        return rows[pl.ds(pl.multiple_of(g * width, width), width), :]

    def lanes(ref, g):
        return ref.at[pl.ds(pl.multiple_of(g * lines, lines), lines), :]

    def users(g):
        return pl.ds(pl.multiple_of(g * UG, UG), UG)

    def by_interest(value):
        return [value[k * UG : (k + 1) * UG] for k in range(interests)]

    def gathered(ref, g):
        return jnp.concatenate([ref[k, users(g), :] for k in range(interests)], axis=0).astype(BF16)

    def put_pooled(g, value):
        for k, part in enumerate(by_interest(value)):
            pooled[k, users(g), :] = part

    def mask_of(g):
        owner = lax.broadcasted_iota(jnp.int32, (UG, width), 0)
        lane = lax.broadcasted_iota(jnp.int32, (UG, width), 1)
        alive = jnp.broadcast_to(live[pl.ds(g, 1), :], (UG, width))
        return (lane // LP == owner) & (alive > 0.0)

    def coupling(value, g):
        powers = [jnp.exp(part) for part in by_interest(value)]
        scale = 1.0 / functools.reduce(jnp.add, powers)
        mask = mask_of(g)
        return jnp.concatenate([jnp.where(mask, p * scale, 0.0) for p in powers], axis=0)

    def coupling_grad(weights, dots):
        ws, ds = by_interest(weights), by_interest(dots)
        inner = functools.reduce(jnp.add, [w * d for w, d in zip(ws, ds)])
        return jnp.concatenate([w * (d - inner) for w, d in zip(ws, ds)], axis=0)

    def loop(count, body):
        lax.fori_loop(0, count, lambda i, c: (body(i), c)[1], 0)

    def over_groups(stages, unroll=16):
        def body(i):
            ids = [i * unroll + j for j in range(unroll)]
            held = [() for _ in ids]
            for stage_fn in stages:
                held = [stage_fn(g, *h) for g, h in zip(ids, held)]

        loop(groups // unroll, body)

    def mapping(k):
        return bilinear[:, k * feature : (k + 1) * feature]

    def squash(summed):
        size = jnp.sum(summed * summed, axis=1, keepdims=True)
        root = jnp.sqrt(size + EPS)
        return size, root, root / (1.0 + size)

    def forward(keep, out):
        for k in range(interests):
            summed = jnp.dot(pooled[k].astype(BF16), mapping(k), preferred_element_type=F32)
            keep[k] = summed
            _, _, factor = squash(summed)
            out[k] = nt((summed * factor).astype(BF16), mapping(k))

    def squash_grad(summed, given):
        size, root, factor = squash(summed)
        along = jnp.sum(summed * given, axis=1, keepdims=True)
        above = 1.0 + size
        slope = 1.0 / (root * above) - 2.0 * root / (above * above)
        return given * factor + summed * (slope * along), factor

    def backward(keep, out):
        for k in range(interests):
            given = jnp.dot(pooled[k].astype(BF16), mapping(k), preferred_element_type=F32)
            grad, _ = squash_grad(keep[k], given)
            out[k] = nt(grad.astype(BF16), mapping(k))

    split_dense = 1024
    parts = narrow_sems.shape[0]
    share = fetched.shape[0] // parts

    def share_of(c):
        return pl.ds(pl.multiple_of(c * share, share), share)

    def copy_in(c):
        return pltpu.make_async_copy(fetched.at[share_of(c), :], narrow.at[share_of(c), :], narrow_sems.at[c])

    def copy_out(c):
        return pltpu.make_async_copy(narrow.at[share_of(c), :], slot_grads.at[share_of(c), :], narrow_sems.at[c])

    loop(parts, lambda c: copy_in(c).start())

    def widen(c):
        copy_in(c).wait()
        for p in range(share // split_dense):
            at = pl.ds(pl.multiple_of(c * share + p * split_dense, split_dense), split_dense)
            wide[at, :] = narrow[at, :].astype(F32)

    loop(parts, widen)
    for stage in (stage_a, stage_b):
        stage[...] = jnp.zeros_like(stage)

    def line_of(g, j):
        return two(slots.at[pl.ds(j * groups, groups)][g])

    def place(j):
        return pl.ds(2 * (j // hist_len * LP + j % hist_len), 2)

    behaviors = UG * hist_len

    def gather(g, stage):
        for j in range(behaviors):
            stage[place(j), :] = wide[line_of(g, j), :]

    def first(g, stage):
        at = pl.ds(pl.multiple_of(g * width, width), width)
        dense = jnp.concatenate(
            [stage[pl.ds(h, width, stride=2), :].astype(BF16) for h in range(2)], axis=1
        )
        rows[at, :] = dense
        start = jnp.concatenate(
            [
                jnp.broadcast_to(first_logits[pl.ds(g * interests + k, 1), :], (UG, width))
                for k in range(interests)
            ],
            axis=0,
        )
        lanes(logits, g)[...] = start
        weights = coupling(start, g)
        lanes(w0, g)[...] = weights
        put_pooled(g, jnp.dot(weights.astype(BF16), dense, preferred_element_type=F32))

    gather(0, stage_a)

    def first_pair(i):
        gather(2 * i + 1, stage_b)
        first(2 * i, stage_a)
        gather(jnp.minimum(2 * i + 2, groups - 1), stage_a)
        first(2 * i + 1, stage_b)

    loop(groups // 2, first_pair)
    forward(s0, q0)

    def turn(q, w, last):
        def agree(g):
            return (nt(gathered(q, g), block(g)),)

        def reweigh(g, scores):
            value = lanes(logits, g)[...] + scores
            if not last:
                lanes(logits, g)[...] = value
            weights = coupling(value, g)
            lanes(w, g)[...] = weights
            return (weights.astype(BF16),)

        def pool(g, weights):
            put_pooled(g, jnp.dot(weights, block(g), preferred_element_type=F32))
            return ()

        over_groups([agree, reweigh, pool])

    turn(q0, w1, False)
    forward(s1, q1)
    turn(q1, w2, True)

    for k in range(interests):
        summed = jnp.dot(pooled[k].astype(BF16), mapping(k), preferred_element_type=F32)
        grad, factor = squash_grad(summed, cotangent[k])
        final[:, k, :] = summed * factor
        g2[k] = nt(grad.astype(BF16), mapping(k))

    for u in range(0, final.shape[0], 64):
        capsules[u : u + 64] = final[u : u + 64].astype(BF16)

    def turn_back(gr, w, z, add):
        def dots(g):
            return (nt(gathered(gr, g), block(g)),)

        def reweigh(g, value):
            grad = coupling_grad(lanes(w, g)[...], value)
            if add:
                grad = grad + lanes(logits, g)[...]
            else:
                lanes(logits, g)[...] = grad
            grad = grad.astype(BF16)
            lanes(z, g)[...] = grad
            return (grad,)

        def pool(g, grad):
            put_pooled(g, jnp.dot(grad, block(g), preferred_element_type=F32))
            return ()

        over_groups([dots, reweigh, pool])

    turn_back(g2, w2, z1, False)
    backward(s1, g1)
    turn_back(g1, w1, z0, True)
    backward(s0, g0)

    def clear(c):
        at = pl.ds(pl.multiple_of(c * split_dense, split_dense), split_dense)
        for total in (wide, more):
            total[at, :] = jnp.zeros((split_dense, HALF), F32)

    loop(fetched.shape[0] // split_dense, clear)

    def spread(g, stage):
        coefs = jnp.concatenate(
            [lanes(w, g)[...].astype(BF16) for w in (w0, w1, w2)]
            + [lanes(z, g)[...] for z in (z0, z1)],
            axis=0,
        )
        basis = jnp.concatenate([gathered(b, g) for b in (g0, g1, g2, q0, q1)], axis=0)
        grads = tn(coefs, basis).astype(BF16)
        part = width // 2
        for p in range(2):
            key = keys[pl.ds(2 * g + p, 1), :]
            column = jnp.transpose(jnp.broadcast_to(key, (UG, part)))[:, :1]
            merged = jnp.dot(
                jnp.where(column == key, 1.0, 0.0).astype(BF16),
                grads[p * part : (p + 1) * part],
                preferred_element_type=F32,
            )
            for h in range(2):
                stage[pl.ds(2 * p * part + h, part, stride=2), :] = merged[:, h * HALF : (h + 1) * HALF]

    def scatter(g, stage):
        add_lines(
            (wide, more),
            behaviors,
            BATCH,
            lambda j: line_of(g, j),
            lambda j: stage[place(j), :],
        )

    spread(0, stage_a)

    def last_pair(i):
        scatter(2 * i, stage_a)
        spread(2 * i + 1, stage_b)
        scatter(2 * i + 1, stage_b)
        spread(jnp.minimum(2 * i + 2, groups - 1), stage_a)

    loop(groups // 2, last_pair)

    def emit(c):
        for p in range(share // split_dense):
            at = pl.ds(pl.multiple_of(c * share + p * split_dense, split_dense), split_dense)
            narrow[at, :] = (wide[at, :] + more[at, :]).astype(BF16)
        copy_out(c).start()

    loop(parts, emit)
    loop(parts, lambda c: copy_out(c).wait())


def route(slots, fetched, bilinear, lengths, init_logits, interest_grad):
    users_here, hist_len, interests = init_logits.shape
    feature = bilinear.shape[0]
    groups = users_here // UG
    width = UG * LP
    pad = LP - hist_len
    batch = jnp.arange(hist_len, dtype=jnp.int32) + hist_len * (jnp.arange(users_here) % 4)[:, None]
    batch = batch // BATCH
    keys = (slots * (4 * LP) + batch).astype(F32)
    keys = jnp.pad(keys, ((0, 0), (0, pad)), constant_values=-1.0).reshape(-1, 4 * LP)
    live = (jnp.arange(LP, dtype=jnp.int32)[None, :] < lengths[:, None]).astype(F32)
    live = live.reshape(groups, width)
    first_logits = jnp.pad(jnp.transpose(init_logits, (0, 2, 1)), ((0, 0), (0, 0), (0, pad)))
    first_logits = first_logits.reshape(groups, UG, interests, LP)
    first_logits = jnp.transpose(first_logits, (0, 2, 1, 3)).reshape(groups * interests, width)
    cotangent = jnp.transpose(interest_grad, (1, 0, 2))
    lines = groups * interests * UG
    lines_of = (2 * slots).reshape(groups, UG * hist_len).T.reshape(-1)
    per_user = pltpu.VMEM((interests, users_here, feature), F32)
    hbm = pl.BlockSpec(memory_space=pltpu.HBM)
    capsules, slot_grads = pl.pallas_call(
        functools.partial(route_kernel, interests, hist_len),
        name="route_users",
        out_shape=(
            jax.ShapeDtypeStruct((users_here, interests, feature), BF16),
            jax.ShapeDtypeStruct(fetched.shape, BF16),
        ),
        in_specs=[smem(), hbm] + [vmem()] * 5,
        out_specs=(vmem(), hbm),
        scratch_shapes=[
            pltpu.VMEM(fetched.shape, BF16),
            pltpu.SemaphoreType.DMA((8,)),
            pltpu.VMEM(fetched.shape, F32),
            pltpu.VMEM(fetched.shape, F32),
            pltpu.VMEM((users_here * LP, feature), BF16),
            pltpu.VMEM((2 * width, HALF), F32),
            pltpu.VMEM((2 * width, HALF), F32),
        ]
        + [pltpu.VMEM((lines, width), F32)] * 4
        + [pltpu.VMEM((lines, width), BF16)] * 2
        + [per_user] * 8
        + [pltpu.VMEM((users_here, interests, feature), F32)],
        compiler_params=pltpu.CompilerParams(vmem_limit_bytes=61 * MIB),
    )(lines_of, fetched, bilinear, first_logits, live, cotangent, keys)
    return capsules, slot_grads


def local(sizes, item_table, bilinear, requests, history, lengths, init_logits, interest_grad):
    asked = requests[0]
    owners, slots = asked.shape
    table_rows = item_table.shape[0]
    fetched, wanted = fetch_rows(asked[:, None, :], item_table, sizes, slots)
    wanted = jnp.where(wanted >= 0, 2 * wanted, 2 * table_rows)
    fetched = fetched.reshape(-1, HALF)
    capsules, slot_grads = route(history, fetched, bilinear, lengths, init_logits, interest_grad)
    returned = exchange(slot_grads.reshape(owners, 2 * slots, HALF), sizes).reshape(-1, HALF)
    return capsules, return_rows(wanted[:, 0, :], returned, table_rows, slots)


def solution(mesh):
    both = ("gx", "gy")
    placed = (
        P(both, None),
        P(),
        P(both, None, None),
        P(both, None),
        P(both),
        P(both, None, None),
        P(both, None, None),
    )
    return jax.shard_map(
        functools.partial(local, (mesh.shape["gx"], mesh.shape["gy"])),
        mesh=mesh,
        in_specs=placed,
        out_specs=(P(both, None, None), P(both, None)),
        check_vma=False,
    )
```
